32 devices in a mesh: dp: 8 (over z, y), tensor: 4 (over x, core).
Axes of the slice: x: 2, y: 2, z: 4, core: 2. Of those that a mesh axis runs over, the one named last changes fastest.
Arguments:
- patches: bfloat16 [64, 24, 24, 1024], P(('dp', 'tensor')), may hold values from -6 to 6
- early_reduce: bfloat16 [1024, 256], replicated, may hold values from -0.1875 to 0.1875
- early_gain_one: float32 [256], replicated, may hold values from 0.5 to 1.5
- early_bias_one: float32 [256], replicated, may hold values from -2.5 to 2.5
- early_kernel: bfloat16 [3, 3, 256, 256], replicated, may hold values from -0.125 to 0.125
- early_gain_two: float32 [256], replicated, may hold values from 0.5 to 1.5
- early_bias_two: float32 [256], replicated, may hold values from -2.5 to 2.5
- early_expand: bfloat16 [256, 1024], replicated, may hold values from -0.375 to 0.375
- early_gain_three: float32 [1024], replicated, may hold values from 0.5 to 1.5
- early_bias_three: float32 [1024], replicated, may hold values from -2.5 to 2.5
- late_reduce: bfloat16 [1024, 256], replicated, may hold values from -0.1875 to 0.1875
- late_gain_one: float32 [256], replicated, may hold values from 0.5 to 1.5
- late_bias_one: float32 [256], replicated, may hold values from -2.5 to 2.5
- late_kernel: bfloat16 [3, 3, 256, 256], replicated, may hold values from -0.125 to 0.125
- late_gain_two: float32 [256], replicated, may hold values from 0.5 to 1.5
- late_bias_two: float32 [256], replicated, may hold values from -2.5 to 2.5
- late_expand: bfloat16 [256, 1024], replicated, may hold values from -0.375 to 0.375
- late_gain_three: float32 [1024], replicated, may hold values from 0.5 to 1.5
- late_bias_three: float32 [1024], replicated, may hold values from -2.5 to 2.5
- readin_weight: bfloat16 [1024, 4096], P(None, 'tensor'), may hold values from -0.1875 to 0.1875
- readin_bias: bfloat16 [4096], P('tensor'), may hold values from -2.5 to 2.5
- readout_weight: bfloat16 [4096, 4096], P('tensor'), may hold values from -0.09375 to 0.09375
- readout_bias: bfloat16 [4096], replicated, may hold values from -2.5 to 2.5
- cotangent: bfloat16 [9216, 4096], P(('dp', 'tensor')), may hold values from -6 to 6
- span_start: int32 [64], P(('dp', 'tensor')), may hold values from 0 to 144, as said below
Outputs:
- projected: bfloat16 [9216, 4096], P(('dp', 'tensor'))
- grad_patches: float32 [64, 24, 24, 1024], P(('dp', 'tensor'))
- grad_early_reduce: float32 [1024, 256], replicated
- grad_early_gain_one: float32 [256], replicated
- grad_early_bias_one: float32 [256], replicated
- grad_early_kernel: float32 [3, 3, 256, 256], replicated
- grad_early_gain_two: float32 [256], replicated
- grad_early_bias_two: float32 [256], replicated
- grad_early_expand: float32 [256, 1024], replicated
- grad_early_gain_three: float32 [1024], replicated
- grad_early_bias_three: float32 [1024], replicated
- grad_late_reduce: float32 [1024, 256], replicated
- grad_late_gain_one: float32 [256], replicated
- grad_late_bias_one: float32 [256], replicated
- grad_late_kernel: float32 [3, 3, 256, 256], replicated
- grad_late_gain_two: float32 [256], replicated
- grad_late_bias_two: float32 [256], replicated
- grad_late_expand: float32 [256, 1024], replicated
- grad_late_gain_three: float32 [1024], replicated
- grad_late_bias_three: float32 [1024], replicated
- grad_readin_weight: float32 [1024, 4096], P(None, 'tensor')
- grad_readin_bias: float32 [4096], P('tensor')
- grad_readout_weight: float32 [4096, 4096], P('tensor')
- grad_readout_bias: float32 [4096], replicated
The draws below stay inside these ranges and needn't reach their ends.
Inputs may be any that keep to these rules, and one draw needn't show every extreme that they name: `span_start`: within each group of 2 consecutive images the offsets are 144 times a permutation of 0 to 1.
All inputs are finite; a program needn't handle non-finite values.
Results may differ from the reference program's by a relative error of at most 0.02.
Values may be sent and summed in bfloat16 or wider, within the bound.
A program may use at most 256 MiB of HBM per device.

```python
import jax
import jax.numpy as jnp
from jax import lax

C = 1024
M = 256
HID = 4096
OUT = 4096
GRID = 24
IMG_DEV = 2
SPAN = 144
IMAGES = 64
ROWS = 9216


def draw_span_start(key, part):
    groups = IMAGES // IMG_DEV
    scores = jax.random.randint(key, (groups, IMG_DEV), 0, 1 << 20) * IMG_DEV + jnp.arange(IMG_DEV, dtype=jnp.int32)[None, :]
    orders = jnp.argsort(scores, axis=1).astype(jnp.int32)
    return (orders * SPAN).reshape(-1).astype(jnp.int32)


def shard_levels(rng, dims, cuts, low, largest):
    def one(axis_at, shards_of):
        heights = jax.random.uniform(jax.random.fold_in(jax.random.fold_in(rng, 6), axis_at), (shards_of,), jnp.float32, low / len(cuts), largest / len(cuts))
        return jnp.repeat(jnp.exp(heights), dims[axis_at] // shards_of).reshape((-1,) + (1,) * (len(dims) - axis_at - 1))

    level = one(*cuts[0])
    for cut in cuts[1:]:
        level = level * one(*cut)
    return level


def noise(rng, shape, scale, reach, pieces=(), kind=jnp.bfloat16):
    level = shard_levels(rng, shape, pieces, -0.22, 0.18) if pieces else 1.0
    array = jax.random.normal(rng, shape, jnp.float32) * scale * level
    return jnp.minimum(jnp.maximum(array, -reach), reach).astype(kind)


def setup_inputs(seed: int = 0) -> dict:
    arg_keys = jax.random.split(jax.random.key(seed), 26)
    patches = noise(arg_keys[0], (IMAGES, GRID, GRID, C), 1.0, 6.0, ((0, 32),))
    early_reduce = noise(arg_keys[1], (C, M), C ** -0.5, 0.1875)
    early_gain_one = jnp.clip(1.0 + 0.1 * jax.random.normal(arg_keys[2], (M,), jnp.float32), 0.5, 1.5)
    early_bias_one = noise(arg_keys[3], (M,), 0.2, 2.5, (), jnp.float32)
    early_kernel = noise(arg_keys[4], (3, 3, M, M), (9 * M) ** -0.5, 0.125)
    early_gain_two = jnp.clip(1.0 + 0.1 * jax.random.normal(arg_keys[5], (M,), jnp.float32), 0.5, 1.5)
    early_bias_two = noise(arg_keys[6], (M,), 0.2, 2.5, (), jnp.float32)
    early_expand = noise(arg_keys[7], (M, C), M ** -0.5, 0.375)
    early_gain_three = jnp.clip(1.0 + 0.1 * jax.random.normal(arg_keys[8], (C,), jnp.float32), 0.5, 1.5)
    early_bias_three = noise(arg_keys[9], (C,), 0.2, 2.5, (), jnp.float32)
    late_reduce = noise(arg_keys[10], (C, M), C ** -0.5, 0.1875)
    late_gain_one = jnp.clip(1.0 + 0.1 * jax.random.normal(arg_keys[11], (M,), jnp.float32), 0.5, 1.5)
    late_bias_one = noise(arg_keys[12], (M,), 0.2, 2.5, (), jnp.float32)
    late_kernel = noise(arg_keys[13], (3, 3, M, M), (9 * M) ** -0.5, 0.125)
    late_gain_two = jnp.clip(1.0 + 0.1 * jax.random.normal(arg_keys[14], (M,), jnp.float32), 0.5, 1.5)
    late_bias_two = noise(arg_keys[15], (M,), 0.2, 2.5, (), jnp.float32)
    late_expand = noise(arg_keys[16], (M, C), M ** -0.5, 0.375)
    late_gain_three = jnp.clip(1.0 + 0.1 * jax.random.normal(arg_keys[17], (C,), jnp.float32), 0.5, 1.5)
    late_bias_three = noise(arg_keys[18], (C,), 0.2, 2.5, (), jnp.float32)
    readin_weight = noise(arg_keys[19], (C, HID), C ** -0.5, 0.1875, ((1, 4),))
    readin_bias = noise(arg_keys[20], (HID,), 0.2, 2.5, ((0, 4),))
    readout_weight = noise(arg_keys[21], (HID, OUT), HID ** -0.5, 0.09375, ((0, 4),))
    readout_bias = noise(arg_keys[22], (OUT,), 0.2, 2.5)
    cotangent = noise(arg_keys[23], (ROWS, OUT), 1.0, 6.0, ((0, 32),))
    span_start = draw_span_start(jax.random.fold_in(arg_keys[25], 71), 0)
    return {"patches": patches, "early_reduce": early_reduce, "early_gain_one": early_gain_one, "early_bias_one": early_bias_one, "early_kernel": early_kernel, "early_gain_two": early_gain_two, "early_bias_two": early_bias_two, "early_expand": early_expand, "early_gain_three": early_gain_three, "early_bias_three": early_bias_three, "late_reduce": late_reduce, "late_gain_one": late_gain_one, "late_bias_one": late_bias_one, "late_kernel": late_kernel, "late_gain_two": late_gain_two, "late_bias_two": late_bias_two, "late_expand": late_expand, "late_gain_three": late_gain_three, "late_bias_three": late_bias_three, "readin_weight": readin_weight, "readin_bias": readin_bias, "readout_weight": readout_weight, "readout_bias": readout_bias, "cotangent": cotangent, "span_start": span_start}


@jax.custom_vjp
def low(v):
    return lax.optimization_barrier(v.astype(jnp.bfloat16)).astype(jnp.float32)

@jax.custom_vjp
def low_back(v):
    return v

def low_keep(v):
    return (low(v), None)

def low_pass(kept, grad):
    return (grad,)

def back_keep(v):
    return (v, None)

def back_low(kept, grad):
    return (low(grad),)
low.defvjp(low_keep, low_pass)
low_back.defvjp(back_keep, back_low)
norm_eps = 1e-06
highest = lax.Precision.HIGHEST

def norm_act(values, gain, shift, active):
    center = values - lax.optimization_barrier(jnp.mean(values, axis=-1, keepdims=True))
    spread = lax.optimization_barrier(jnp.mean(center * center, axis=-1, keepdims=True))
    normed = center * lax.rsqrt(spread + norm_eps) * gain + shift
    if active:
        return jax.nn.silu(normed)
    return normed

def block(values, params):
    reduce_weight, gain_one, bias_one, kernel, gain_two, bias_two, expand_weight, gain_three, bias_three = params
    reduced = low_back(jnp.einsum('nhwc,cm->nhwm', low(values), reduce_weight, precision=highest))
    activated = low(norm_act(reduced, gain_one, bias_one, True))
    convolved = low_back(lax.conv_general_dilated(activated, kernel, (1, 1), ((1, 1), (1, 1)), dimension_numbers=('NHWC', 'HWIO', 'NHWC'), precision=highest))
    middle = low(norm_act(convolved, gain_two, bias_two, True))
    expanded = low_back(jnp.einsum('nhwm,mc->nhwc', middle, expand_weight, precision=highest))
    return values + norm_act(expanded, gain_three, bias_three, False)

def forward(patches, early, late, readin_weight, readin_bias, readout_weight, readout_bias):
    early_out = block(patches, early)
    images, side = (early_out.shape[0], early_out.shape[1])
    half = side // 2
    pooled = lax.optimization_barrier(jnp.mean(early_out.reshape(images, half, 2, half, 2, early_out.shape[-1]), axis=(2, 4)))
    late_out = block(pooled, late)
    tokens = low(late_out).reshape(-1, late_out.shape[-1])
    hidden_pre = low_back(jnp.dot(tokens, readin_weight, precision=highest) + readin_bias)
    active = low(jax.nn.gelu(hidden_pre, approximate=True))
    return jnp.dot(active, readout_weight, precision=highest) + readout_bias

def reference(patches, early_reduce, early_gain_one, early_bias_one, early_kernel, early_gain_two, early_bias_two, early_expand, early_gain_three, early_bias_three, late_reduce, late_gain_one, late_bias_one, late_kernel, late_gain_two, late_bias_two, late_expand, late_gain_three, late_bias_three, readin_weight, readin_bias, readout_weight, readout_bias, cotangent, span_start):
    early = tuple((item.astype(jnp.float32) for item in (early_reduce, early_gain_one, early_bias_one, early_kernel, early_gain_two, early_bias_two, early_expand, early_gain_three, early_bias_three)))
    late = tuple((item.astype(jnp.float32) for item in (late_reduce, late_gain_one, late_bias_one, late_kernel, late_gain_two, late_bias_two, late_expand, late_gain_three, late_bias_three)))
    result, pull = jax.vjp(forward, patches.astype(jnp.float32), early, late, readin_weight.astype(jnp.float32), readin_bias.astype(jnp.float32), readout_weight.astype(jnp.float32), readout_bias.astype(jnp.float32))
    starts = jnp.arange(IMAGES, dtype=jnp.int32) // IMG_DEV * (IMG_DEV * SPAN) + span_start.astype(jnp.int32)
    packed_rows = (starts[:, None] + jnp.arange(SPAN, dtype=jnp.int32)[None, :]).reshape(-1)
    projected = jnp.zeros((IMAGES * SPAN, OUT), jnp.bfloat16).at[packed_rows].set(result.astype(jnp.bfloat16))
    grads = pull(cotangent[packed_rows].astype(jnp.float32))
    grad_patches, grad_early, grad_late, grad_readin, grad_readin_bias, grad_readout, grad_readout_bias = grads
    return (projected, grad_patches, grad_early[0], grad_early[1], grad_early[2], grad_early[3], grad_early[4], grad_early[5], grad_early[6], grad_early[7], grad_early[8], grad_late[0], grad_late[1], grad_late[2], grad_late[3], grad_late[4], grad_late[5], grad_late[6], grad_late[7], grad_late[8], grad_readin, grad_readin_bias, grad_readout, grad_readout_bias)
```

```python
from functools import partial

import jax
import jax.numpy as jnp
from jax import lax
from jax.sharding import PartitionSpec as P

norm_eps = 1e-06


def norm_act(values, gain, shift, active):
    center = values - jnp.mean(values, axis=-1, keepdims=True)
    spread = jnp.mean(center * center, axis=-1, keepdims=True)
    normed = center * lax.rsqrt(spread + norm_eps) * gain + shift
    if active:
        return jax.nn.silu(normed)
    return normed


def norm_pull(values, gain, shift, active, grad):
    _, pull = jax.vjp(
        lambda inner_in, gain_in, shift_in: norm_act(inner_in, gain_in, shift_in, active),
        values,
        gain,
        shift,
    )
    return pull(grad)


def contract_rows(left, right):
    return lax.dot_general(
        left, right, (((0,), (0,)), ((), ())), preferred_element_type=jnp.float32
    )


def contract_cols(left, right):
    return lax.dot_general(
        left, right, (((1,), (1,)), ((), ())), preferred_element_type=jnp.float32
    )


def patches_of(values):
    images, grid_side = (values.shape[0], values.shape[1])
    padded = jnp.pad(values, ((0, 0), (1, 1), (1, 1), (0, 0)))
    pieces = [
        padded[:, row_off : row_off + grid_side, col_off : col_off + grid_side, :]
        for row_off in range(3)
        for col_off in range(3)
    ]
    return jnp.concatenate(pieces, axis=-1).reshape(
        images * grid_side * grid_side, 9 * values.shape[-1]
    )


def block_forward(values, params):
    (
        reduce_weight,
        gain_one,
        bias_one,
        kernel,
        gain_two,
        bias_two,
        expand_weight,
        gain_three,
        bias_three,
    ) = params
    images, grid_side, _, channels = values.shape
    lowered = values.astype(jnp.bfloat16).reshape(-1, channels)
    reduced = jnp.dot(lowered, reduce_weight, preferred_element_type=jnp.float32)
    activated = norm_act(reduced, gain_one, bias_one, True).astype(jnp.bfloat16)
    columns = patches_of(activated.reshape(images, grid_side, grid_side, -1))
    convolved = jnp.dot(
        columns, kernel.reshape(-1, kernel.shape[-1]), preferred_element_type=jnp.float32
    )
    middle = norm_act(convolved, gain_two, bias_two, True).astype(jnp.bfloat16)
    expanded = jnp.dot(middle, expand_weight, preferred_element_type=jnp.float32)
    output = values + norm_act(expanded, gain_three, bias_three, False).reshape(values.shape)
    return (output, (lowered, reduced, columns, convolved, middle, expanded))


def block_backward(grad_out, saved, params):
    (
        reduce_weight,
        gain_one,
        bias_one,
        kernel,
        gain_two,
        bias_two,
        expand_weight,
        gain_three,
        bias_three,
    ) = params
    lowered, reduced, columns, convolved, middle, expanded = saved
    images, grid_side, _, channels = grad_out.shape
    grad_flat = grad_out.reshape(-1, channels)
    grad_expanded, grad_gain_three, grad_bias_three = norm_pull(
        expanded, gain_three, bias_three, False, grad_flat
    )
    grad_expanded = grad_expanded.astype(jnp.bfloat16)
    grad_expand = contract_rows(middle, grad_expanded)
    grad_middle = contract_cols(grad_expanded, expand_weight)
    grad_convolved, grad_gain_two, grad_bias_two = norm_pull(
        convolved, gain_two, bias_two, True, grad_middle
    )
    grad_convolved = grad_convolved.astype(jnp.bfloat16)
    width_mid = kernel.shape[-1]
    grad_kernel = contract_rows(columns, grad_convolved).reshape(kernel.shape)
    flipped = jnp.transpose(kernel[::-1, ::-1], (0, 1, 3, 2)).reshape(-1, width_mid)
    grad_activated = jnp.dot(
        patches_of(grad_convolved.reshape(images, grid_side, grid_side, width_mid)),
        flipped,
        preferred_element_type=jnp.float32,
    )
    grad_reduced, grad_gain_one, grad_bias_one = norm_pull(
        reduced, gain_one, bias_one, True, grad_activated
    )
    grad_reduced = grad_reduced.astype(jnp.bfloat16)
    grad_reduce = contract_rows(lowered, grad_reduced)
    grad_input = grad_flat + contract_cols(grad_reduced, reduce_weight)
    return (
        grad_input.reshape(grad_out.shape),
        (
            grad_reduce,
            grad_gain_one,
            grad_bias_one,
            grad_kernel,
            grad_gain_two,
            grad_bias_two,
            grad_expand,
            grad_gain_three,
            grad_bias_three,
        ),
    )


RING_LINES = 4


def ring_order(size):
    lines = RING_LINES if size % RING_LINES == 0 else 1
    width = size // lines
    if lines == 1 or width == 1:
        return list(range(size))
    order = []
    for line in range(lines):
        cols = range(1, width) if line % 2 == 0 else range(width - 1, 0, -1)
        order += [line * width + col for col in cols]
    return order + [line * width for line in range(lines - 1, -1, -1)]


def shift_tensor(values, hop):
    size = lax.axis_size("tensor")
    return lax.ppermute(values, "tensor", [(i, (i + hop) % size) for i in range(size)])


def swap_core(values):
    size = lax.axis_size("tensor")
    return lax.ppermute(values, "tensor", [(i, i ^ 1) for i in range(size)])


def gather_group(values):
    chips = lax.axis_size("tensor") // 2
    blocks, moved = [], values
    for hop in range(chips):
        if hop:
            moved = shift_tensor(moved, 2)
        blocks += [moved, swap_core(moved)]
    return jnp.concatenate(blocks, axis=0)


def scatter_group(values):
    chips = lax.axis_size("tensor") // 2
    parts = values.reshape(chips, 2, -1, values.shape[-1])
    paired = [
        (parts[hop, 0].astype(jnp.float32) + swap_core(parts[hop, 1]).astype(jnp.float32))
        for hop in range(chips)
    ]
    total = paired[chips - 1]
    for hop in range(chips - 2, -1, -1):
        moved = shift_tensor(total.astype(jnp.bfloat16), -2)
        total = moved.astype(jnp.float32) + paired[hop]
    return total


def ring_sum(values):
    size = lax.axis_size("dp")
    if size > 8:
        return lax.psum(values, "dp").astype(jnp.float32)
    order = ring_order(size)
    place = jnp.array([order.index(i) for i in range(size)], jnp.int32)[lax.axis_index("dp")]
    ahead = [(order[i], order[(i + 1) % size]) for i in range(size)]
    back = [(b, a) for a, b in ahead]
    rows, cols = values.shape
    pieces = values.reshape(2, size, rows // (2 * size), cols)
    turns = ((ahead, 1), (back, -1))
    moving = [lax.dynamic_index_in_dim(pieces[i], place, 0, False) for i in range(2)]
    for step in range(size - 1):
        for i, (pairs, sign) in enumerate(turns):
            got = lax.ppermute(moving[i], "dp", pairs)
            at = (place - sign * (step + 1) + 2 * size) % size
            mine = lax.dynamic_index_in_dim(pieces[i], at, 0, False)
            moving[i] = (got.astype(jnp.float32) + mine.astype(jnp.float32)).astype(jnp.bfloat16)
    out = jnp.zeros((2, size) + pieces.shape[2:], jnp.float32)
    for step in range(size):
        for i, (pairs, sign) in enumerate(turns):
            at = (place - sign * (step - 1) + 2 * size) % size
            out = lax.dynamic_update_slice(
                out, moving[i].astype(jnp.float32)[None, None], (i, at, 0, 0)
            )
            if step < size - 1:
                moving[i] = lax.ppermute(moving[i], "dp", pairs)
    return out.reshape(rows, cols)


def sum_all(flat):
    chips = lax.axis_size("tensor") // 2
    low = flat.astype(jnp.bfloat16)
    core = lax.axis_index("tensor") % 2
    halves = low.reshape(2, -1, low.shape[-1])
    mine = lax.dynamic_index_in_dim(halves, core, 0, False).astype(jnp.float32)
    total = mine + swap_core(lax.dynamic_index_in_dim(halves, 1 - core, 0, False)).astype(jnp.float32)
    moved = total.astype(jnp.bfloat16)
    for hop in range(chips - 1):
        moved = shift_tensor(moved, 2)
        total = total + moved.astype(jnp.float32)
    total = ring_sum(total.astype(jnp.bfloat16)).astype(jnp.bfloat16)
    other = swap_core(total)
    first = jnp.where(core == 0, total, other)
    second = jnp.where(core == 0, other, total)
    return jnp.concatenate([first, second], axis=0).astype(jnp.float32)


def shards(
    patches,
    early_reduce,
    early_gain_one,
    early_bias_one,
    early_kernel,
    early_gain_two,
    early_bias_two,
    early_expand,
    early_gain_three,
    early_bias_three,
    late_reduce,
    late_gain_one,
    late_bias_one,
    late_kernel,
    late_gain_two,
    late_bias_two,
    late_expand,
    late_gain_three,
    late_bias_three,
    readin_weight,
    readin_bias,
    readout_weight,
    readout_bias,
    cotangent,
    span_start,
):
    early = (
        early_reduce,
        early_gain_one,
        early_bias_one,
        early_kernel,
        early_gain_two,
        early_bias_two,
        early_expand,
        early_gain_three,
        early_bias_three,
    )
    late = (
        late_reduce,
        late_gain_one,
        late_bias_one,
        late_kernel,
        late_gain_two,
        late_bias_two,
        late_expand,
        late_gain_three,
        late_bias_three,
    )
    images, grid_side, _, channels = patches.shape
    early_out, early_saved = block_forward(patches.astype(jnp.float32), early)
    half = grid_side // 2
    pooled = jnp.mean(early_out.reshape(images, half, 2, half, 2, channels), axis=(2, 4))
    late_out, late_saved = block_forward(pooled, late)
    span = half * half
    tokens = late_out.astype(jnp.bfloat16).reshape(images * span, channels)
    rows_here = tokens.shape[0]
    placing = (span_start[:, None] == span * jnp.arange(images, dtype=jnp.int32)[None, :]).astype(
        jnp.bfloat16
    )
    gelu_tanh = partial(jax.nn.gelu, approximate=True)
    gathered = gather_group(tokens)
    hidden_pre = jnp.dot(
        gathered, readin_weight, preferred_element_type=jnp.float32
    ) + readin_bias.astype(jnp.float32)
    active = gelu_tanh(hidden_pre).astype(jnp.bfloat16)
    result = scatter_group(
        jnp.dot(active, readout_weight, preferred_element_type=jnp.float32).astype(jnp.bfloat16)
    ) + readout_bias.astype(jnp.float32)
    result_low = result.astype(jnp.bfloat16).reshape(images, span, -1)
    projected = (
        jnp.einsum("ij,itk->jtk", placing, result_low, preferred_element_type=jnp.float32)
        .astype(jnp.bfloat16)
        .reshape(rows_here, -1)
    )
    grad_result = (
        jnp.einsum(
            "ij,jtk->itk",
            placing,
            cotangent.reshape(images, span, -1),
            preferred_element_type=jnp.float32,
        )
        .astype(jnp.bfloat16)
        .reshape(rows_here, -1)
    )
    grad_readout_bias = jnp.sum(grad_result.astype(jnp.float32), axis=0)
    all_grads = gather_group(grad_result)
    grad_readout = ring_sum(contract_rows(active, all_grads).astype(jnp.bfloat16))
    grad_active = contract_cols(all_grads, readout_weight)
    _, gelu_pull = jax.vjp(gelu_tanh, hidden_pre)
    grad_hidden = gelu_pull(grad_active)[0].astype(jnp.bfloat16)
    grad_readin_bias = jnp.sum(grad_hidden.astype(jnp.float32), axis=0)
    grad_readin = ring_sum(contract_rows(gathered, grad_hidden).astype(jnp.bfloat16))
    grad_tokens = scatter_group(contract_cols(grad_hidden, readin_weight).astype(jnp.bfloat16))
    grad_late_out = grad_tokens.reshape(images, half, half, channels)
    grad_pooled, late_grads = block_backward(grad_late_out, late_saved, late)
    grad_early_out = jnp.repeat(jnp.repeat(grad_pooled * 0.25, 2, axis=1), 2, axis=2)
    grad_patches, early_grads = block_backward(grad_early_out, early_saved, early)
    grads = list(early_grads) + list(late_grads) + [grad_readout_bias]
    chunk = 32 * lax.axis_size("dp") * channels
    flat = jnp.concatenate([item.reshape(-1) for item in grads])
    flat = jnp.pad(flat, (0, -flat.size % (2 * chunk)))
    flat = sum_all(flat.reshape(-1, channels)).reshape(-1)
    summed, start = [], 0
    for item in grads:
        summed.append(flat[start : start + item.size].reshape(item.shape))
        start += item.size
    grad_readin_bias = lax.psum(grad_readin_bias, "dp")
    return (
        projected,
        grad_patches,
        summed[0],
        summed[1],
        summed[2],
        summed[3],
        summed[4],
        summed[5],
        summed[6],
        summed[7],
        summed[8],
        summed[9],
        summed[10],
        summed[11],
        summed[12],
        summed[13],
        summed[14],
        summed[15],
        summed[16],
        summed[17],
        grad_readin,
        grad_readin_bias,
        grad_readout,
        summed[18],
    )


def solution(mesh):
    in_specs = (
        P(("dp", "tensor"), None, None, None),
        P(),
        P(),
        P(),
        P(),
        P(),
        P(),
        P(),
        P(),
        P(),
        P(),
        P(),
        P(),
        P(),
        P(),
        P(),
        P(),
        P(),
        P(),
        P(None, "tensor"),
        P("tensor"),
        P("tensor", None),
        P(),
        P(("dp", "tensor"), None),
        P(("dp", "tensor")),
    )
    out_specs = (
        P(("dp", "tensor"), None),
        P(("dp", "tensor"), None, None, None),
        P(),
        P(),
        P(),
        P(),
        P(),
        P(),
        P(),
        P(),
        P(),
        P(),
        P(),
        P(),
        P(),
        P(),
        P(),
        P(),
        P(),
        P(),
        P(None, "tensor"),
        P("tensor"),
        P("tensor", None),
        P(),
    )
    return jax.shard_map(shards, mesh=mesh, in_specs=in_specs, out_specs=out_specs, check_vma=False)
```

```python
from functools import partial

import jax
import jax.numpy as jnp
from jax import lax
from jax.experimental import pallas as pl
from jax.experimental.pallas import tpu as pltpu
from jax.sharding import PartitionSpec as P

norm_eps = 1e-06
MESH = pl.DeviceIdType.MESH
f32, bf16 = jnp.float32, jnp.bfloat16


def dot(left, right):
    return jnp.dot(left, right, preferred_element_type=f32)


def dot_nt(left, right):
    return lax.dot_general(left, right, (((1,), (1,)), ((), ())), preferred_element_type=f32)


def dot_tn(left, right):
    return lax.dot_general(left, right, (((0,), (0,)), ((), ())), preferred_element_type=f32)


def two_part(left, right):
    high = right.astype(bf16)
    rest = (right - high.astype(f32)).astype(bf16)
    return dot(left, high) + dot(left, rest)


def ones_where(same):
    return jnp.where(same, 1.0, 0.0).astype(bf16)


def iota(shape, dim):
    return lax.broadcasted_iota(jnp.int32, shape, dim)


def hat(values):
    center = values - jnp.mean(values, axis=-1, keepdims=True)
    scale = lax.rsqrt(jnp.mean(center * center, axis=-1, keepdims=True) + norm_eps)
    return center * scale, scale


def sigmoid(v):
    return 1.0 / (1.0 + jnp.exp(-v))


def norm_back(hatted, scale, grad):
    inner = jnp.mean(grad * hatted, axis=-1, keepdims=True)
    return scale * (grad - jnp.mean(grad, axis=-1, keepdims=True) - hatted * inner)


def column_sum(values):
    return jnp.sum(values, axis=0, keepdims=True)


class Grid:
    def __init__(self, images, side, width):
        self.images, self.side, self.width = images, side, width
        self.stride = -(-side // 8) * 8
        self.lines = 8 if side % 8 == 0 else side
        self.chunk = self.lines * self.stride
        self.per_image = side // self.lines
        self.rows = images * side * self.stride
        self.chunks = self.rows // self.chunk
        self.tall = (side + 1) * self.stride
        self.padded = images * self.tall + self.stride
        self.full = self.stride == side

    def here(self, index):
        return pl.ds(pl.multiple_of(index * self.chunk, 8), self.chunk)

    def at(self, index):
        return index // self.per_image * self.tall + index % self.per_image * self.chunk + self.stride

    def bordered(self, index, line=0):
        return pl.ds(pl.multiple_of(self.at(index) + line * self.stride, 8), self.chunk)

    def cells_only(self, values):
        if self.full:
            return values
        return jnp.where(iota(values.shape, 0) % self.stride < self.side, values, 0.0)


def clear_borders(grid, spread):
    for image in range(grid.images + 1):
        border = pl.ds(image * grid.tall, grid.stride)
        spread[border, 0 : 3 * grid.width] = jnp.zeros((grid.stride, 3 * grid.width), f32)


def spread_columns(grid, spread):
    width, size = grid.width, grid.chunk

    def one(i, _):
        start = pl.multiple_of(grid.at(i) - 8, 8)
        middle = spread[pl.ds(start, size + 16), width : 2 * width]
        left = pltpu.roll(middle, 1, 0)[8 : 8 + size]
        right = pltpu.roll(middle, size + 15, 0)[8 : 8 + size]
        if grid.full:
            column = iota((size, width), 0) % grid.stride
            left = jnp.where(column == 0, 0.0, left)
            right = jnp.where(column == grid.side - 1, 0.0, right)
        spread[grid.bordered(i), 0:width] = left
        spread[grid.bordered(i), 2 * width : 3 * width] = right
        return 0

    lax.fori_loop(0, grid.chunks, one, 0)


def block_forward(grid, load, params, reduced, convolved, spread, emit):
    weight, gain1, bias1, kernel, gain2, bias2, expand, gain3, bias3 = params
    width = grid.width
    clear_borders(grid, spread)

    def first(i, _):
        value = dot(load(i).astype(bf16), weight[...])
        reduced[grid.here(i), :] = value
        normed = hat(value)[0] * gain1[...] + bias1[...]
        low = (normed * sigmoid(normed)).astype(bf16).astype(f32)
        spread[grid.bordered(i), width : 2 * width] = grid.cells_only(low)
        return 0

    lax.fori_loop(0, grid.chunks, first, 0)
    spread_columns(grid, spread)

    def second(i, _):
        total = dot(spread[grid.bordered(i, -1), 0 : 3 * width].astype(bf16), kernel[0])
        total += dot(spread[grid.bordered(i, 0), 0 : 3 * width].astype(bf16), kernel[1])
        total += dot(spread[grid.bordered(i, 1), 0 : 3 * width].astype(bf16), kernel[2])
        convolved[grid.here(i), :] = total
        normed = hat(total)[0] * gain2[...] + bias2[...]
        expanded = dot((normed * sigmoid(normed)).astype(bf16), expand[...])
        emit(i, load(i).astype(f32) + hat(expanded)[0] * gain3[...] + bias3[...])
        return 0

    lax.fori_loop(0, grid.chunks, second, 0)


def block_backward(grid, load, load_grad, params, reduced, convolved, spread, grads, emit):
    weight, gain1, bias1, kernel, gain2, bias2, expand, gain3, bias3 = params
    d_weight, d_gain1, d_bias1, d_kernel, d_gain2, d_bias2, d_expand, d_gain3, d_bias3 = grads
    width = grid.width
    for ref in grads:
        ref[...] = jnp.zeros(ref.shape, f32)
    clear_borders(grid, spread)

    def first(i, _):
        hat2, scale2 = hat(convolved[grid.here(i), :])
        normed = hat2 * gain2[...] + bias2[...]
        sig = sigmoid(normed)
        middle = (normed * sig).astype(bf16)
        hat3, scale3 = hat(dot(middle, expand[...]))
        grad = load_grad(i)
        d_gain3[...] += column_sum(grad * hat3)
        d_bias3[...] += column_sum(grad)
        grad_expanded = norm_back(hat3, scale3, grad * gain3[...]).astype(bf16)
        d_expand[...] += dot_tn(middle, grad_expanded)
        grad_normed = dot_nt(grad_expanded, expand[...]) * (sig * (1.0 + normed * (1.0 - sig)))
        d_gain2[...] += column_sum(grad_normed * hat2)
        d_bias2[...] += column_sum(grad_normed)
        grad_convolved = norm_back(hat2, scale2, grad_normed * gain2[...])
        spread[grid.bordered(i), width : 2 * width] = grad_convolved.astype(bf16).astype(f32)
        return 0

    lax.fori_loop(0, grid.chunks, first, 0)
    spread_columns(grid, spread)
    yield

    def second(i, _):
        hat1, scale1 = hat(reduced[grid.here(i), :])
        normed = hat1 * gain1[...] + bias1[...]
        sig = sigmoid(normed)
        active = grid.cells_only(normed * sig).astype(bf16)
        total = None
        for line in range(3):
            moved = spread[grid.bordered(i, line - 1), 0 : 3 * width].astype(bf16)
            part = dot_tn(active, moved)
            for col in range(3):
                cols = slice(col * width, (col + 1) * width)
                tap = (2 - line) * 3 + 2 - col
                d_kernel[tap * width : (tap + 1) * width, :] += part[:, cols]
                back = kernel[2 - line, (2 - col) * width : (3 - col) * width, :]
                product = dot_nt(moved[:, cols], back)
                total = product if total is None else total + product
        grad_normed = grid.cells_only(total * (sig * (1.0 + normed * (1.0 - sig))))
        d_gain1[...] += column_sum(grad_normed * hat1)
        d_bias1[...] += column_sum(grad_normed)
        grad_reduced = norm_back(hat1, scale1, grad_normed * gain1[...]).astype(bf16)
        d_weight[...] += dot_tn(load(i).astype(bf16), grad_reduced)
        emit(i, load_grad(i) + dot_nt(grad_reduced, weight[...]))
        return 0

    lax.fori_loop(0, grid.chunks, second, 0)


def pool_matrix(early, late, down):
    cells = early.lines // 2 * late.stride
    shape = (cells, early.chunk) if down else (early.chunk, cells)
    big, small = iota(shape, 1 if down else 0), iota(shape, 0 if down else 1)
    same_line = big // (2 * early.stride) == small // late.stride
    return ones_where(same_line & (big % early.stride // 2 == small % late.stride))


def token_matrix(late, starts, first, rows, down):
    shape = (rows, late.rows) if down else (late.chunk, rows)
    packed, cell = iota(shape, 0 if down else 1), iota(shape, 1 if down else 0)
    if down:
        packed += first
    else:
        cell += first
    inside = cell % (late.side * late.stride)
    line, column = inside // late.stride, inside % late.stride
    image = cell // (late.side * late.stride)
    start = jnp.zeros(shape, jnp.int32)
    for n in range(late.images):
        start = jnp.where(image == n, starts[n], start)
    return ones_where((packed == start + line * late.side + column) & (column < late.side))


PIECES = 16
RING = 8
RING_LINES = 4


class Plan:
    def __init__(self, images, side, channels, width, group, ring, hidden, out):
        self.early, self.late = Grid(images, side, width), Grid(images, side // 2, width)
        self.images, self.channels, self.width, self.out = images, channels, width, out
        self.span = (side // 2) ** 2
        self.block = images * self.span
        self.group, self.chips = group, group // 2
        self.rows = group * self.block
        self.ring = ring == RING and group == 4
        self.hidden = hidden
        self.piece = out // PIECES
        self.slab = channels // PIECES
        taps = 9 * width
        self.kernel_at = (0, taps)
        self.reduce_at = (2 * taps, 2 * taps + channels)
        self.expand_at = (2 * taps + 2 * channels, 2 * taps + 3 * channels)
        self.small_at = 2 * taps + 4 * channels
        self.small_block = 4 + 2 * channels // width
        self.small = 2 * self.small_block + out // width + group * hidden // width
        self.flat_piece = -(-(self.small_at + self.small) // (group * PIECES * 16)) * 16
        self.flat = group * PIECES * self.flat_piece


def ring_place(device):
    line, column = device // 2, lax.rem(device, 2)
    return (1 - column) * line + column * (2 * RING_LINES - 1 - line)


def ring_device(place):
    column = place // RING_LINES
    return 2 * ((1 - column) * place + column * (2 * RING_LINES - 1 - place)) + column


class Ring:
    def __init__(self, place, held, first, out, sems, local, tap=None):
        self.place, self.held, self.first, self.out = place, held, first, out
        self.sems, self.local, self.tap = sems, local, tap
        ahead = ring_device(lax.rem(place + 1, RING))
        behind = ring_device(lax.rem(place + RING - 1, RING))
        self.to = (ahead, behind)

    def index(self, way, step):
        turn = self.place - step if way == 0 else self.place + step
        return way * RING + lax.rem(turn + 2 * RING, RING)

    def copy(self, way, step, gather):
        if gather:
            target = self.out.at[self.index(way, step - 1)]
            source = self.held.at[way, RING - 2] if step == 0 else target
        else:
            source = self.first.at[way] if step == 0 else self.held.at[way, step - 1]
            target = self.held.at[way, step]
        return pltpu.make_async_remote_copy(
            src_ref=source,
            dst_ref=target,
            send_sem=self.sems[2 * gather].at[way, step],
            recv_sem=self.sems[2 * gather + 1].at[way, step],
            device_id={"dp": self.to[way]},
            device_id_type=MESH,
        )

    def keep(self, way):
        target = self.out.at[self.index(way, -1)]
        return pltpu.make_async_copy(self.held.at[way, RING - 2], target, self.local.at[way])

    def reduce(self, step, partial):
        for way in range(2):
            if step:
                self.copy(way, step - 1, 0).wait_recv()
            target = self.first.at[way] if step == 0 else self.held.at[way, step - 1]

            def put(window, value, target=target):
                if step:
                    value = value + target[window].astype(f32)
                target[window] = value.astype(bf16)

            partial(way, self.index(way, step), put)
            if step < RING - 1:
                self.copy(way, step, 0).start()
            else:
                self.copy(way, 0, 1).start()
                self.keep(way).start()
                if self.tap:
                    self.tap(way, 0, self.index(way, -1), self.held.at[way, RING - 2])

    def gather(self, step):
        for way in range(2):
            copy = self.copy(way, step - 1, 1)
            copy.wait_recv()
            index = self.index(way, step - 1)
            if step < RING - 1:
                self.copy(way, step, 1).start()
            if self.tap:
                self.tap(way, step, index, self.out.at[index])

    def tick(self, count, partial):
        if count < RING:
            self.reduce(count, partial)
        else:
            self.gather(count - RING + 1)

    def finish(self):
        for way in range(2):
            self.keep(way).wait()
            for step in range(RING - 1):
                self.copy(way, step, 0).wait_send()
                self.copy(way, step, 1).wait_send()


TICKS = 2 * RING - 1


def mega(plan, names, *all_refs):
    r = dict(zip(names, all_refs))
    early, late, block, chips, group = plan.early, plan.late, plan.block, plan.chips, plan.group
    hid, out, piece, ch, width = plan.hidden, plan.out, plan.piece, plan.channels, plan.width
    me = lax.axis_index("tensor")
    chip, core = me // 2, lax.rem(me, 2)
    place = ring_place(lax.axis_index("dp")) if plan.ring else 0 * me
    pair = {"tensor": 2 * chip + 1 - core}
    ep, lp = ([r[f"{name}{k}"] for k in range(9)] for name in ("early", "late"))

    def other(hop):
        return {"tensor": 2 * lax.rem(chip + hop + chips, chips) + core}

    started = []

    def send(source, target, name, at, device):
        return pltpu.make_async_remote_copy(
            src_ref=source,
            dst_ref=target,
            send_sem=r[name + "_s"].at[at],
            recv_sem=r[name + "_r"].at[at],
            device_id=device,
            device_id_type=MESH,
        )

    def go(copy, keep=True):
        copy.start()
        if keep:
            started.append(copy)

    def order(step):
        back, forth = lax.rem(place - step + 2 * RING, RING), lax.rem(place + step, RING)
        return (back, RING + forth)

    def columns(index, size):
        return pl.ds(pl.multiple_of(index * size, 128), size)

    def rows_at(index, size):
        return pl.ds(pl.multiple_of(index * size, 16), size)

    sems = [r[f"ring_{kind}"] for kind in ("rs", "rr", "gs", "gr")]

    def ring_of(n, held, first, target, tap=None):
        mine = [sem.at[n] for sem in sems]
        return Ring(place, held, first, target, mine, r["ring_l"].at[n], tap)

    gflat = r["gflat"]

    def spread_piece(way, step, index, source):
        for hop in range(1, chips):
            go(send(source, gflat.at[core, chip, index], "ax", (hop - 1, way, step), other(hop)))

    one = ring_of(0, r["held"], r["first"], r["gout"])
    two = ring_of(1, r["held2"], r["first2"], r["gin"])
    three = ring_of(2, r["held3"], r["first3"], gflat.at[core, chip], spread_piece) if plan.ring else None

    barrier = pltpu.get_barrier_semaphore()
    friends = [pair] + [other(hop) for hop in range(1, chips)]
    if plan.ring:
        friends += [{"dp": one.to[0]}, {"dp": one.to[1]}]
    for friend in friends:
        pl.semaphore_signal(barrier, inc=1, device_id=friend, device_id_type=MESH)
    pl.semaphore_wait(barrier, len(friends))

    cot, gall = r["cot"], r["gall"]

    def cot_own(step):
        for way, index in enumerate(order(step)):
            go(send(cot.at[:, columns(index, piece)], gall.at[1, index], "cc", (0, step, way), pair))

    def cot_far(step):
        for hop in range(1, chips):
            for way, index in enumerate(order(step)):
                source = cot.at[:, columns(index, piece)]
                go(send(source, gall.at[2 * hop, index], "cx", (hop - 1, step, way), other(hop)))

    def cot_pass(step):
        for hop in range(1, chips):
            for way, index in enumerate(order(step)):
                source = gall.at[2 * hop, index]
                send(source, source, "cx", (hop - 1, step, way), other(hop)).wait_recv()
                go(send(source, gall.at[2 * hop + 1, index], "cc", (hop, step, way), pair))

    ready = set()

    def cot_ready(step):
        if step in ready:
            return
        ready.add(step)
        for hop in range(chips):
            for way, index in enumerate(order(step)):
                target = gall.at[2 * hop + 1, index]
                send(target, target, "cc", (hop, step, way), pair).wait_recv()

    fetch = pltpu.make_async_copy(r["x"], r["xs"], r["load"].at[0])
    fetch.start()
    for step in range(3):
        cot_far(step)
    for step in range(RING):
        cot_own(step)
    fetch.wait()

    xs, pool, act, tok, big = r["xs"], r["pool"], r["act"], r["tok"], r["big"]
    cells = early.lines // 2 * late.stride

    def load_early(i):
        return xs[early.here(i), :]

    def load_late(i):
        return pool[late.here(i), :]

    def put_early(i, value):
        pool[rows_at(i, cells), :] = two_part(pool_matrix(early, late, True), value) * 0.25

    tsend, tpair, tfar = r["tsend"], r["tpair"], r["tfar"]

    def put_late(i, value):
        tsend[i, 0 : late.chunk, :] = value.astype(bf16)

    block_forward(early, load_early, ep, r["ered"], r["econv"], big, put_early)
    block_forward(late, load_late, lp, r["lred"], r["lconv"], big, put_late)
    for n in range(plan.images):
        matrix = token_matrix(late, r["starts"], n * plan.span, plan.span, True)
        value = None
        for i in range(late.chunks):
            part = dot(matrix[:, i * late.chunk : (i + 1) * late.chunk], tsend[i, 0 : late.chunk, :])
            value = part if value is None else value + part
        tok[0, n * plan.span : (n + 1) * plan.span, :] = value.astype(bf16)
    token_sends = [send(tok.at[0], tok.at[2 * hop], "tx", (hop - 1,), other(hop)) for hop in range(1, chips)]
    token_sends.append(send(tok.at[0], tok.at[1], "tc", (0,), pair))
    for copy in token_sends:
        copy.start()
    for step in range(3, RING):
        cot_far(step)
    for step in range(3):
        cot_pass(step)

    slope, win = r["slope"], r["win"]

    def hidden_of(j):
        half = block // 2

        def body(i, _):
            pre = dot(tok[j, rows_at(i, half), :], win[...]) + r["bin"][...]
            bend = jnp.tanh(0.7978845608 * (pre + 0.044715 * pre * pre * pre))
            rows = rows_at(2 * j + i, half)
            act[rows, :] = (0.5 * pre * (1.0 + bend)).astype(bf16)
            rise = 0.7978845608 * (1.0 + 3.0 * 0.044715 * pre * pre)
            slope[rows, :] = (0.5 * (1.0 + bend) + 0.5 * pre * (1.0 - bend * bend) * rise).astype(bf16)
            return 0

        lax.fori_loop(0, 2, body, 0)

    hidden_of(0)
    send(tok.at[0], tok.at[1], "tc", (0,), pair).wait_recv()
    hidden_of(1)
    for hop in range(1, chips):
        send(tok.at[0], tok.at[2 * hop], "tx", (hop - 1,), other(hop)).wait_recv()
        token_sends.append(send(tok.at[2 * hop], tok.at[2 * hop + 1], "tc", (hop,), pair))
        token_sends[-1].start()
        hidden_of(2 * hop)
        send(tok.at[0], tok.at[2 * hop + 1], "tc", (hop,), pair).wait_recv()
        hidden_of(2 * hop + 1)

    turned, gbuf = r["turned"], r["gbuf"]

    def turn(i, _):
        stripe = act[:, columns(i, 128)].astype(f32)
        turned[rows_at(i, 128), :] = jnp.transpose(stripe).astype(bf16)
        return 0

    lax.fori_loop(0, hid // 128, turn, 0)

    def cot_piece(j, index):
        return cot.at[:, columns(index, piece)] if j == 0 else gall.at[j, index]

    def piece_loads(step, way):
        slot, index = step % 2, order(step)[way]
        loads = []
        for j in range(group):
            target = gbuf.at[slot, way, pl.ds(j * block, block), :]
            loads.append(pltpu.make_async_copy(cot_piece(j, index), target, r["gload"].at[slot, way, j]))
        return loads

    def prepare(step):
        cot_ready(step)
        for way in range(2):
            for load in piece_loads(step, way):
                load.start()

    def piece_of(step):
        def partial(way, index, put):
            for load in piece_loads(step, way):
                load.wait()
            tile = gbuf.at[step % 2, way]
            r["outbias"][pl.ds(index, 1), :] = column_sum(tile[0:block, :].astype(f32))

            def body(i, _):
                rows = rows_at(i, 256)
                put((rows, slice(None)), dot(turned[rows, :], tile[...]))
                return 0

            lax.fori_loop(0, hid // 256, body, 0)

        return partial

    def alone(step, ring, partial):
        for way, index in enumerate(order(step)):
            stage = ring.first.at[way]

            def put(window, value, stage=stage):
                stage[window] = value.astype(bf16)

            partial(way, index, put)
            write = pltpu.make_async_copy(stage, ring.out.at[index], ring.local.at[way])
            write.start()
            write.wait()

    def tick(ring, count, partial):
        if plan.ring:
            ring.tick(count, partial)
        elif count < RING:
            alone(count, ring, partial)

    def tick_one(count):
        tick(one, count, piece_of(count))
        if count + 1 < RING:
            prepare(count + 1)

    wout, wbuf, rbuf = r["wout"], r["wbuf"], r["rbuf"]
    tiles = out // piece

    def result_pass(blocks, extra, finish):
        def loads(i, slot):
            cols = columns(i, piece)
            pairs = [(wout.at[:, cols], wbuf.at[slot, pl.ds(0, hid), pl.ds(0, piece)])]
            for n, ref in enumerate(extra):
                pairs.append((ref.at[:, cols], wbuf.at[slot, pl.ds(n * block, block), pl.ds(piece, piece)]))
            return [pltpu.make_async_copy(a, b, r["wload"].at[slot, n]) for n, (a, b) in enumerate(pairs)]

        for load in loads(0, 0):
            load.start()

        def body(i, _):
            slot = lax.rem(i, 2)
            for load in loads(i, slot):
                load.wait()

            @pl.when(i + 1 < tiles)
            def _():
                for load in loads(i + 1, 1 - slot):
                    load.start()

            for n, j in enumerate(blocks):
                value = dot(act[j * block : (j + 1) * block, :], wbuf[slot, 0:hid, 0:piece])
                for m in range(len(extra)):
                    value += wbuf[slot, m * block : (m + 1) * block, piece : 2 * piece].astype(f32)
                finish(n, i, value)
            return 0

        lax.fori_loop(0, tiles, body, 0)

    def pair_copy(hop):
        return send(rbuf.at[hop], r["rpair"].at[hop], "rp", (hop,), pair)

    def result_pairs():
        def put(n, i, value):
            rbuf[n, :, columns(i, piece)] = value.astype(bf16)

        result_pass([2 * hop + 1 for hop in range(chips)], [], put)
        for hop in range(chips):
            go(pair_copy(hop), False)

    def result_pairs_done():
        for hop in range(chips):
            pair_copy(hop).wait()

    def result_far():
        for hop in range(chips - 1, 0, -1):
            extra = [r["rpair"].at[hop]]
            if hop < chips - 1:
                send(rbuf.at[0], r["rfar"].at[hop], "rx", (hop,), other(-1)).wait_recv()
                extra.append(r["rfar"].at[hop])

            def put(n, i, value, hop=hop):
                rbuf[hop, :, columns(i, piece)] = value.astype(bf16)

            result_pass([2 * hop], extra, put)
            go(send(rbuf.at[hop], r["rfar"].at[hop - 1], "rx", (hop - 1,), other(-1)))

    def result_own():
        send(rbuf.at[0], r["rfar"].at[0], "rx", (0,), other(-1)).wait_recv()

        def put(n, i, value):
            cols = columns(i, piece)
            rbuf[0, :, cols] = (value + r["bout"][:, cols]).astype(bf16)

        result_pass([0], [r["rpair"].at[0], r["rfar"].at[0]], put)
        go(pltpu.make_async_copy(rbuf.at[0], r["projected"], r["load"].at[1]))

    def active_loads(step, slot):
        loads = []
        for way, index in enumerate(order(step)):
            for j in range(group):
                target = rbuf.at[slot, :, pl.ds((way * group + j) * piece, piece)]
                sem = r["aload"].at[slot, way, j]
                loads.append(pltpu.make_async_copy(cot_piece(j, index), target, sem))
            target = wbuf.at[slot, pl.ds(0, hid), pl.ds(way * piece, piece)]
            sem = r["aload"].at[slot, way, group]
            loads.append(pltpu.make_async_copy(wout.at[:, columns(index, piece)], target, sem))
        return loads

    def active_steps(low, high):
        for load in active_loads(low, low % 2):
            load.start()

        def body(step, _):
            slot = lax.rem(step, 2)
            for load in active_loads(step, slot):
                load.wait()

            @pl.when(step + 1 < high)
            def _():
                for load in active_loads(step + 1, 1 - slot):
                    load.start()

            def rows_of(j, _):
                rows = rows_at(j, block)
                value = dot_nt(rbuf[slot, :, columns(j, piece)], wbuf[slot, 0:hid, 0:piece])
                value += dot_nt(rbuf[slot, :, columns(group + j, piece)], wbuf[slot, 0:hid, piece : 2 * piece])
                before = big[rows, 0:hid]
                big[rows, 0:hid] = value + (jnp.where(step == 0, 0.0, before) if low == 0 else before)
                return 0

            lax.fori_loop(0, group, rows_of, 0)
            return 0

        lax.fori_loop(low, high, body, 0)

    def hidden_back():
        r["inbias"][...] = jnp.zeros(r["inbias"].shape, f32)

        def body(i, _):
            rows = rows_at(i, block // 2)
            value = (big[rows, 0:hid] * slope[rows, :].astype(f32)).astype(bf16)
            slope[rows, :] = value
            r["inbias"][...] += column_sum(value.astype(f32))
            return 0

        lax.fori_loop(0, 2 * group, body, 0)

    def tokens_back(j):
        return dot_nt(slope[j * block : (j + 1) * block, :], win[...])

    def tokens_pair(hop):
        return send(tsend.at[hop], tpair.at[hop], "gc", (hop,), pair)

    def tokens_far_copy(hop):
        return send(tsend.at[hop], tfar.at[hop - 1], "gx_", (hop - 1,), other(-1))

    def fetched(source, target):
        load = pltpu.make_async_copy(source, target, r["load"].at[2])
        load.start()
        load.wait()
        return target[...].astype(f32)

    def tokens_far():
        for hop in range(chips - 1, -1, -1):
            tsend[hop] = tokens_back(2 * hop + 1).astype(bf16)
            go(tokens_pair(hop), False)
        for hop in range(chips - 1, 0, -1):
            value = tokens_back(2 * hop)
            tokens_pair(hop).wait()
            value = value + fetched(tpair.at[hop], tsend.at[hop])
            if hop < chips - 1:
                tokens_far_copy(hop + 1).wait_recv()
                value = value + fetched(tfar.at[hop], tsend.at[hop])
            tsend[hop] = value.astype(bf16)
            go(tokens_far_copy(hop))

    def tokens_own():
        value = tokens_back(0)
        tokens_pair(0).wait()
        value = value + fetched(tpair.at[0], tsend.at[0])
        tokens_far_copy(1).wait_recv()
        value = value + fetched(tfar.at[0], tsend.at[0])
        high = value.astype(bf16)
        tsend[0] = high
        rest = (value - high.astype(f32)).astype(bf16)
        for i in range(late.chunks):
            matrix = token_matrix(late, r["starts"], i * late.chunk, block, False)
            r["gpool"][i * late.chunk : (i + 1) * late.chunk, :] = dot(matrix, tsend[0]) + dot(matrix, rest)

    parts = hid // 256

    def weights_in():
        for copy in token_sends:
            copy.wait_send()

        def body(i, _):
            total = None
            for j in range(group):
                part = dot_tn(tok[j, :, columns(i, 256)], slope[j * block : (j + 1) * block, :])
                total = part if total is None else total + part
            for q in range(parts):
                tok[q, 0:256, columns(i, 256)] = total[:, q * 256 : (q + 1) * 256].astype(bf16)
            return 0

        lax.fori_loop(0, ch // 256, body, 0)

    def slab_of(way, index, put):
        each = 256 // plan.slab
        for q in range(parts):
            value = tok[q, rows_at(lax.rem(index, each), plan.slab), columns(index // each, 256)]
            put((slice(None), slice(q * 256, (q + 1) * 256)), value.astype(f32))

    def tick_two(count):
        tick(two, count, slab_of)

    gpool, flat = r["gpool"], r["flat"]
    acc = [r[f"acc{k}"] for k in range(9)]

    def late_back():
        def put(i, value):
            gpool[late.here(i), :] = value * 0.25

        def grad(i):
            return gpool[late.here(i), :]

        return block_backward(late, load_late, grad, lp, r["lred"], r["lconv"], big, acc, put)

    def early_back():
        def grad(i):
            return two_part(pool_matrix(early, late, False), gpool[rows_at(i, cells), :])

        def put(i, value):
            xs[early.here(i), :] = value.astype(bf16)

        return block_backward(early, load_early, grad, ep, r["ered"], r["econv"], big, acc, put)

    small = r["small"]

    def store_flat(n):
        flat[pl.ds(plan.kernel_at[n], 9 * width), :] = acc[3][...].astype(bf16)
        flat[pl.ds(plan.reduce_at[n], ch), :] = acc[0][...].astype(bf16)
        quarters = ch // width
        for q in range(quarters):
            rows = pl.ds(plan.expand_at[n] + q * width, width)
            flat[rows, :] = acc[6][:, q * width : (q + 1) * width].astype(bf16)
        at = n * plan.small_block
        for k, ref in enumerate((acc[1], acc[2], acc[4], acc[5])):
            small[at + k : at + k + 1, :] = ref[...]
        for k, ref in enumerate((acc[7], acc[8])):
            for q in range(quarters):
                row = at + 4 + k * quarters + q
                small[row : row + 1, :] = ref[:, q * width : (q + 1) * width]

    def store_small():
        at = 2 * plan.small_block
        small[at : at + out // width, :] = r["outbias"][...]
        at += out // width
        for owner in range(group):
            for q in range(hid // width):
                row = at + owner * (hid // width) + q
                part = r["inbias"][:, q * width : (q + 1) * width]
                small[row : row + 1, :] = jnp.where(me == owner, part, 0.0)
        row = at + group * hid // width
        small[row:, :] = jnp.zeros((small.shape[0] - row, width), f32)
        flat[pl.ds(plan.small_at, small.shape[0]), :] = small[...].astype(bf16)
        rest = plan.small_at + small.shape[0]
        flat[pl.ds(rest, plan.flat - rest), :] = jnp.zeros((plan.flat - rest, width), bf16)

    half, quarter = plan.flat // 2, plan.flat // group
    flat_piece = plan.flat_piece

    def flat_pair():
        away = flat.at[rows_at(1 - core, half), :]
        return send(away, r["fpair"], "fp", (0,), pair)

    def flat_far_copy(hop):
        return send(gbuf.at[1], r["ffar"], "fx", (hop - 1,), other(hop))

    def own_piece(index):
        across = big.shape[1] // width
        return rows_at(index // across, flat_piece), columns(lax.rem(index, across), width)

    upper = PIECES // 2

    def stage(sources):
        loads = [
            pltpu.make_async_copy(source, gbuf.at[0, n], r["load"].at[2 + n])
            for n, source in enumerate(sources)
        ]
        for load in loads:
            load.start()
        for load in loads:
            load.wait()

    def staged(i):
        return (i // upper, rows_at(lax.rem(i, upper), flat_piece))

    def flat_far():
        flat_pair().wait_recv()
        for hop in range(chips - 1, -1, -1):
            to = lax.rem(chip + hop, chips)
            stage([r["fpair"].at[rows_at(2 * to + n, quarter // 2), :] for n in range(2)])

            def body(i, _, hop=hop, to=to):
                mine = pl.ds(pl.multiple_of(core * half + to * quarter + i * flat_piece, 16), flat_piece)
                total = flat[mine, :].astype(f32) + gbuf[(0, *staged(i))].astype(f32)
                if hop:
                    gbuf[(1, *staged(i))] = total.astype(bf16)
                else:
                    big[own_piece(i)] = total
                return 0

            lax.fori_loop(0, PIECES, body, 0)
            if hop:
                go(flat_far_copy(hop))

    def flat_sum():
        for hop in range(1, chips):
            flat_far_copy(hop).wait_recv()
            stage([r["ffar"].at[n] for n in range(2)])

            def body(i, _):
                big[own_piece(i)] += gbuf[(0, *staged(i))].astype(f32)
                return 0

            lax.fori_loop(0, PIECES, body, 0)

    def flat_of(way, index, put):
        put((slice(None), slice(None)), big[own_piece(index)])

    def tick_three(count):
        tick(three, count, flat_of)

    def flat_spread():
        for hop in range(1, chips):
            theirs = gflat.at[core, lax.rem(chip - hop + chips, chips)]
            for way in range(2):
                for step in range(RING):
                    piece_ref = theirs.at[three.index(way, step - 1)]
                    send(piece_ref, piece_ref, "ax", (hop - 1, way, step), other(hop)).wait_recv()
        three.finish()
        go(send(gflat.at[core], gflat.at[core], "ac", (0,), pair))
        send(gflat.at[core], gflat.at[core], "ac", (0,), pair).wait_recv()

    prepare(0)
    tick_one(0)
    for step in range(3, 5):
        cot_pass(step)
    result_pairs()
    cot_pass(5)
    tick_one(1)
    for step in range(6, RING):
        cot_pass(step)
    for step in range(RING):
        cot_ready(step)
    result_pairs_done()
    active_steps(0, 4)
    tick_one(2)
    active_steps(4, RING)
    tick_one(3)
    hidden_back()
    tokens_far()
    weights_in()
    tick_one(4)
    tick_two(0)
    tokens_own()
    result_far()
    tick_one(5)
    tick_two(1)
    part = late_back()
    next(part)
    for _ in part:
        pass
    store_flat(1)
    tick_one(6)
    tick_two(2)
    part = early_back()
    next(part)
    tick_one(7)
    tick_two(3)
    for _ in part:
        pass
    go(pltpu.make_async_copy(xs, r["gx"], r["load"].at[0]))
    store_flat(0)
    store_small()
    tick_one(8)
    tick_two(4)
    if plan.ring:
        go(flat_pair())
        flat_far()
    else:
        go(pltpu.make_async_copy(flat, r["gflat"], r["load"].at[2]))
    result_own()
    tick_one(9)
    tick_two(5)
    if plan.ring:
        flat_sum()
    for count in range(10, TICKS):
        tick_one(count)
        tick_two(count - 4)
        if plan.ring:
            tick_three(count - 10)
    for count in range(TICKS, TICKS + 4):
        tick_two(count - 4)
        if plan.ring:
            tick_three(count - 10)
    if plan.ring:
        for count in range(TICKS + 4, TICKS + 10):
            tick_three(count - 10)
        flat_spread()
        for ring in (one, two):
            ring.finish()
    for copy in started:
        if copy.is_remote:
            copy.wait_send()
        else:
            copy.wait()


def unpack_body(gout, gin, gx, kernel0, kernel1, reduce0, reduce1, expand0, expand1, small, *outs):
    big_outs, small_outs = outs[:9], outs[9:]
    big_outs[0][...] = gout[0].astype(f32)
    big_outs[1][...] = gin[0].astype(f32)
    for source, target in zip((gx, kernel0, kernel1, reduce0, reduce1, expand0, expand1), big_outs[2:]):
        target[...] = source[...].astype(f32)

    @pl.when(pl.program_id(0) == 0)
    def _():
        row, width = 0, small.shape[1]
        for target in small_outs:
            for q in range(target.shape[1] // width):
                target[:, q * width : (q + 1) * width] = small[row : row + 1, :].astype(f32)
                row += 1


def unpack(plan, gout, gin, gx, flat):
    width, ch, hid, out, group = plan.width, plan.channels, plan.hidden, plan.out, plan.group
    shape = partial(jax.ShapeDtypeStruct, dtype=f32)
    taps, steps = 9 * width, PIECES
    quarters = ch // width
    each = steps // quarters

    def rows_spec(size, start, columns=width):
        assert start % size == 0
        return pl.BlockSpec((size, columns), lambda i: (start // size + i, 0))

    lane = width // each
    in_specs = [
        pl.BlockSpec((1, hid, plan.piece), lambda i: (i, 0, 0)),
        pl.BlockSpec((1, plan.slab, hid), lambda i: (i, 0, 0)),
        rows_spec(plan.early.rows // steps, 0, ch),
        *[rows_spec(taps // steps, plan.kernel_at[n]) for n in range(2)],
        *[rows_spec(ch // steps, plan.reduce_at[n]) for n in range(2)],
        *[rows_spec(lane, plan.expand_at[n]) for n in range(2)],
        pl.BlockSpec((128, width), lambda i: (plan.small_at // 128, 0)),
    ]
    expand_out = pl.BlockSpec((lane, width), lambda i: (i % each, i // each))
    smalls = [width] * 4 + [ch] * 2
    smalls = smalls + smalls + [out, group * hid]
    out_specs = [
        pl.BlockSpec((hid, plan.piece), lambda i: (0, i)),
        rows_spec(plan.slab, 0, hid),
        rows_spec(plan.early.rows // steps, 0, ch),
        *[rows_spec(taps // steps, 0)] * 2,
        *[rows_spec(ch // steps, 0)] * 2,
        *[expand_out] * 2,
        *[pl.BlockSpec((1, size), lambda i: (0, 0)) for size in smalls],
    ]
    out_shape = [shape((hid, out)), shape((ch, hid)), shape((plan.early.rows, ch))]
    out_shape += [shape((taps, width))] * 2 + [shape((ch, width))] * 2 + [shape((width, ch))] * 2
    out_shape += [shape((1, size)) for size in smalls]
    return pl.pallas_call(
        unpack_body, grid=(steps,), in_specs=in_specs, out_specs=out_specs, out_shape=out_shape
    )(gout, gin, gx, *[flat] * 7)


def shards(*args):
    patches, early, late = args[0], args[1:10], args[10:19]
    readin_weight, readin_bias, readout_weight, readout_bias, cotangent, span_start = args[19:]
    images, side, _, channels = patches.shape
    width, hidden, out = early[0].shape[1], readin_weight.shape[1], readout_weight.shape[1]
    group, ring = lax.axis_size("tensor"), lax.axis_size("dp")
    plan = Plan(images, side, channels, width, group, ring, hidden, out)
    chips, block, rows = plan.chips, plan.block, plan.rows

    def matrices(params):
        kernel = params[3].reshape(3, 3 * width, width)
        return [params[0], params[1][None], params[2][None], kernel, params[4][None], params[5][None],
                params[6], params[7][None], params[8][None]]

    inputs = {"starts": span_start, "x": patches.reshape(-1, channels)}
    inputs |= {f"early{k}": item for k, item in enumerate(matrices(early))}
    inputs |= {f"late{k}": item for k, item in enumerate(matrices(late))}
    inputs |= {"win": readin_weight, "bin": readin_bias.astype(f32)[None], "wout": readout_weight,
               "bout": readout_bias.astype(f32)[None], "cot": cotangent}
    quarter = plan.flat // group
    gflat = (2, chips, PIECES, plan.flat_piece, width) if plan.ring else (plan.flat, width)
    outputs = {
        "projected": (block, out),
        "gx": (plan.early.rows, channels),
        "gout": (PIECES, hidden, plan.piece),
        "gin": (PIECES, plan.slab, hidden),
        "gflat": gflat,
        "gall": (group, PIECES, block, plan.piece),
        "rpair": (chips, block, out),
        "rfar": (max(chips - 1, 1), block, out),
        "tpair": (chips, block, channels),
        "tfar": (chips - 1, block, channels),
        "fpair": (plan.flat // 2, width),
        "ffar": (2, quarter // 2, width),
    }
    hops = RING - 1
    early_rows, late_rows = plan.early.rows, plan.late.rows
    low = {
        "xs": (early_rows, channels),
        "tok": (group, block, channels),
        "act": (rows, hidden),
        "slope": (rows, hidden),
        "turned": (hidden, rows),
        "gbuf": (2, 2, rows, plan.piece),
        "held": (2, hops, hidden, plan.piece),
        "first": (2, hidden, plan.piece),
        "wbuf": (2, max(hidden, 2 * block), 2 * plan.piece),
        "rbuf": (chips, block, out),
        "tsend": (chips, block, channels),
        "held2": (2, hops, plan.slab, hidden),
        "first2": (2, plan.slab, hidden),
        "held3": (2, hops, plan.flat_piece, width),
        "first3": (2, plan.flat_piece, width),
        "flat": (plan.flat, width),
    }
    wide = {
        "pool": (late_rows, channels),
        "gpool": (late_rows, channels),
        "ered": (early_rows, width),
        "econv": (early_rows, width),
        "lred": (late_rows, width),
        "lconv": (late_rows, width),
        "big": (max(plan.early.padded, rows), max(3 * width, hidden)),
        "small": (64, width),
        "outbias": (PIECES, plan.piece),
        "inbias": (1, hidden),
        "acc0": (channels, width),
        "acc1": (1, width),
        "acc2": (1, width),
        "acc3": (9 * width, width),
        "acc4": (1, width),
        "acc5": (1, width),
        "acc6": (width, channels),
        "acc7": (1, channels),
        "acc8": (1, channels),
    }
    remote = {
        "cx": (chips - 1, RING, 2),
        "cc": (chips, RING, 2),
        "tx": (chips - 1,),
        "tc": (chips,),
        "rp": (chips,),
        "rx": (chips - 1,),
        "gc": (chips,),
        "gx_": (chips - 1,),
        "fp": (1,),
        "fx": (chips - 1,),
        "ax": (chips - 1, 2, RING),
        "ac": (1,),
    }
    copies = {f"{name}_{end}": size for name, size in remote.items() for end in "sr"}
    copies |= {f"ring_{kind}": (3, 2, hops) for kind in ("rs", "rr", "gs", "gr")}
    copies |= {"ring_l": (3, 2), "load": (4,), "gload": (2, 2, group), "wload": (2, 3), "aload": (2, 2, group + 1)}
    hbm, vmem = pl.BlockSpec(memory_space=pltpu.HBM), pl.BlockSpec(memory_space=pltpu.VMEM)
    kinds = {"starts": pl.BlockSpec(memory_space=pltpu.SMEM), "x": hbm, "wout": hbm, "cot": hbm}
    scratch = [pltpu.VMEM(size, bf16) for size in low.values()]
    scratch += [pltpu.VMEM(size, f32) for size in wide.values()]
    scratch += [pltpu.SemaphoreType.DMA(size) for size in copies.values()]
    names = [*inputs, *outputs, *low, *wide, *copies]
    landed = pl.pallas_call(
        partial(mega, plan, names),
        out_shape=[jax.ShapeDtypeStruct(size, bf16) for size in outputs.values()],
        in_specs=[kinds.get(name, vmem) for name in inputs],
        out_specs=[hbm] * len(outputs),
        scratch_shapes=scratch,
        compiler_params=pltpu.CompilerParams(
            collective_id=0, has_side_effects=True, vmem_limit_bytes=67043328
        ),
    )(*inputs.values())
    projected, grad_x, gout, gin, flat = landed[:5]
    flat = flat.reshape(plan.flat, width)
    if not plan.ring:
        gout, gin = lax.psum(gout, "dp"), lax.psum(gin, "dp")
        flat = lax.psum(flat, ("dp", "tensor"))
    done = unpack(plan, gout, gin, grad_x, flat)
    grad_readout, grad_readin, grad_patches = done[:3]
    kernels, reduces, expands, smalls = done[3:5], done[5:7], done[7:9], done[9:]

    def grads(n):
        small = [item[0] for item in smalls[6 * n : 6 * n + 6]]
        kernel = kernels[n].reshape(3, 3, width, width)
        return [reduces[n], small[0], small[1], kernel, small[2], small[3], expands[n], small[4], small[5]]

    readin_sum = smalls[13][0].reshape(group, hidden)
    grad_readin_bias = lax.dynamic_index_in_dim(readin_sum, lax.axis_index("tensor"), 0, False)
    return (
        projected,
        grad_patches.reshape(patches.shape),
        *grads(0),
        *grads(1),
        grad_readin,
        grad_readin_bias,
        grad_readout,
        smalls[12][0],
    )


def solution(mesh):
    in_specs = (
        P(("dp", "tensor"), None, None, None),
        P(),
        P(),
        P(),
        P(),
        P(),
        P(),
        P(),
        P(),
        P(),
        P(),
        P(),
        P(),
        P(),
        P(),
        P(),
        P(),
        P(),
        P(),
        P(None, "tensor"),
        P("tensor"),
        P("tensor", None),
        P(),
        P(("dp", "tensor"), None),
        P(("dp", "tensor")),
    )
    out_specs = (
        P(("dp", "tensor"), None),
        P(("dp", "tensor"), None, None, None),
        P(),
        P(),
        P(),
        P(),
        P(),
        P(),
        P(),
        P(),
        P(),
        P(),
        P(),
        P(),
        P(),
        P(),
        P(),
        P(),
        P(),
        P(),
        P(None, "tensor"),
        P("tensor"),
        P("tensor", None),
        P(),
    )
    return jax.shard_map(shards, mesh=mesh, in_specs=in_specs, out_specs=out_specs, check_vma=False)
```

```python
from functools import partial

import jax
import jax.numpy as jnp
from jax import lax
from jax.experimental import pallas as pl
from jax.experimental.pallas import tpu as pltpu
from jax.sharding import PartitionSpec as P

norm_eps = 1e-06
MESH = pl.DeviceIdType.MESH
f32, bf16 = jnp.float32, jnp.bfloat16


def dot(left, right):
    return jnp.dot(left, right, preferred_element_type=f32)


def dot_nt(left, right):
    return lax.dot_general(left, right, (((1,), (1,)), ((), ())), preferred_element_type=f32)


def dot_tn(left, right):
    return lax.dot_general(left, right, (((0,), (0,)), ((), ())), preferred_element_type=f32)


def two_part(left, right):
    high = right.astype(bf16)
    rest = (right - high.astype(f32)).astype(bf16)
    return dot(left, high) + dot(left, rest)


def ones_where(same):
    return jnp.where(same, 1.0, 0.0).astype(bf16)


def iota(shape, dim):
    return lax.broadcasted_iota(jnp.int32, shape, dim)


def hat(values):
    center = values - jnp.mean(values, axis=-1, keepdims=True)
    scale = lax.rsqrt(jnp.mean(center * center, axis=-1, keepdims=True) + norm_eps)
    return center * scale, scale


def sigmoid(v):
    return 1.0 / (1.0 + jnp.exp(-v))


def norm_back(hatted, scale, grad):
    inner = jnp.mean(grad * hatted, axis=-1, keepdims=True)
    return scale * (grad - jnp.mean(grad, axis=-1, keepdims=True) - hatted * inner)


def column_sum(values):
    return jnp.sum(values, axis=0, keepdims=True)


class Grid:
    def __init__(self, images, side, width):
        self.images, self.side, self.width = images, side, width
        self.stride = -(-side // 8) * 8
        self.lines = 8 if side % 8 == 0 else side
        self.chunk = self.lines * self.stride
        self.per_image = side // self.lines
        self.rows = images * side * self.stride
        self.chunks = self.rows // self.chunk
        self.tall = (side + 1) * self.stride
        self.padded = images * self.tall + self.stride
        self.full = self.stride == side

    def here(self, index):
        return pl.ds(pl.multiple_of(index * self.chunk, 8), self.chunk)

    def at(self, index):
        return index // self.per_image * self.tall + index % self.per_image * self.chunk + self.stride

    def bordered(self, index, line=0):
        return pl.ds(pl.multiple_of(self.at(index) + line * self.stride, 8), self.chunk)

    def cells_only(self, values):
        if self.full:
            return values
        return jnp.where(iota(values.shape, 0) % self.stride < self.side, values, 0.0)


def clear_borders(grid, spread):
    for image in range(grid.images + 1):
        border = pl.ds(image * grid.tall, grid.stride)
        spread[border, 0 : 3 * grid.width] = jnp.zeros((grid.stride, 3 * grid.width), f32)


def spread_columns(grid, spread):
    width, size = grid.width, grid.chunk

    def one(i, _):
        start = pl.multiple_of(grid.at(i) - 8, 8)
        middle = spread[pl.ds(start, size + 16), width : 2 * width]
        left = pltpu.roll(middle, 1, 0)[8 : 8 + size]
        right = pltpu.roll(middle, size + 15, 0)[8 : 8 + size]
        if grid.full:
            column = iota((size, width), 0) % grid.stride
            left = jnp.where(column == 0, 0.0, left)
            right = jnp.where(column == grid.side - 1, 0.0, right)
        spread[grid.bordered(i), 0:width] = left
        spread[grid.bordered(i), 2 * width : 3 * width] = right
        return 0

    lax.fori_loop(0, grid.chunks, one, 0)


def block_forward(grid, load, params, reduced, convolved, spread, emit):
    weight, gain1, bias1, kernel, gain2, bias2, expand, gain3, bias3 = params
    width = grid.width
    clear_borders(grid, spread)

    def first(i, _):
        value = dot(load(i).astype(bf16), weight[...])
        reduced[grid.here(i), :] = value
        normed = hat(value)[0] * gain1[...] + bias1[...]
        low = (normed * sigmoid(normed)).astype(bf16).astype(f32)
        spread[grid.bordered(i), width : 2 * width] = grid.cells_only(low)
        return 0

    lax.fori_loop(0, grid.chunks, first, 0)
    spread_columns(grid, spread)

    def second(i, _):
        total = dot(spread[grid.bordered(i, -1), 0 : 3 * width].astype(bf16), kernel[0])
        total += dot(spread[grid.bordered(i, 0), 0 : 3 * width].astype(bf16), kernel[1])
        total += dot(spread[grid.bordered(i, 1), 0 : 3 * width].astype(bf16), kernel[2])
        convolved[grid.here(i), :] = total
        normed = hat(total)[0] * gain2[...] + bias2[...]
        expanded = dot((normed * sigmoid(normed)).astype(bf16), expand[...])
        emit(i, load(i).astype(f32) + hat(expanded)[0] * gain3[...] + bias3[...])
        return 0

    lax.fori_loop(0, grid.chunks, second, 0)


def block_backward(grid, load, load_grad, params, reduced, convolved, spread, grads, emit, cuts):
    weight, gain1, bias1, kernel, gain2, bias2, expand, gain3, bias3 = params
    d_weight, d_gain1, d_bias1, d_kernel, d_gain2, d_bias2, d_expand, d_gain3, d_bias3 = grads
    width = grid.width
    for ref in grads:
        ref[...] = jnp.zeros(ref.shape, f32)
    clear_borders(grid, spread)

    def first(i, _):
        hat2, scale2 = hat(convolved[grid.here(i), :])
        normed = hat2 * gain2[...] + bias2[...]
        sig = sigmoid(normed)
        middle = (normed * sig).astype(bf16)
        hat3, scale3 = hat(dot(middle, expand[...]))
        grad = load_grad(i)
        d_gain3[...] += column_sum(grad * hat3)
        d_bias3[...] += column_sum(grad)
        grad_expanded = norm_back(hat3, scale3, grad * gain3[...]).astype(bf16)
        d_expand[...] += dot_tn(middle, grad_expanded)
        grad_normed = dot_nt(grad_expanded, expand[...]) * (sig * (1.0 + normed * (1.0 - sig)))
        d_gain2[...] += column_sum(grad_normed * hat2)
        d_bias2[...] += column_sum(grad_normed)
        grad_convolved = norm_back(hat2, scale2, grad_normed * gain2[...])
        spread[grid.bordered(i), width : 2 * width] = grad_convolved.astype(bf16).astype(f32)
        return 0

    for low, high in cuts[0]:
        lax.fori_loop(low, high, first, 0)
        if high == grid.chunks:
            spread_columns(grid, spread)
        yield

    def second(i, _):
        hat1, scale1 = hat(reduced[grid.here(i), :])
        normed = hat1 * gain1[...] + bias1[...]
        sig = sigmoid(normed)
        active = grid.cells_only(normed * sig).astype(bf16)
        total = None
        for line in range(3):
            moved = spread[grid.bordered(i, line - 1), 0 : 3 * width].astype(bf16)
            part = dot_tn(active, moved)
            for col in range(3):
                cols = slice(col * width, (col + 1) * width)
                tap = (2 - line) * 3 + 2 - col
                d_kernel[tap * width : (tap + 1) * width, :] += part[:, cols]
                back = kernel[2 - line, (2 - col) * width : (3 - col) * width, :]
                product = dot_nt(moved[:, cols], back)
                total = product if total is None else total + product
        grad_normed = grid.cells_only(total * (sig * (1.0 + normed * (1.0 - sig))))
        d_gain1[...] += column_sum(grad_normed * hat1)
        d_bias1[...] += column_sum(grad_normed)
        grad_reduced = norm_back(hat1, scale1, grad_normed * gain1[...]).astype(bf16)
        d_weight[...] += dot_tn(load(i).astype(bf16), grad_reduced)
        emit(i, load_grad(i) + dot_nt(grad_reduced, weight[...]))
        return 0

    for low, high in cuts[1]:
        lax.fori_loop(low, high, second, 0)
        yield


def pool_matrix(early, late, down):
    cells = early.lines // 2 * late.stride
    shape = (cells, early.chunk) if down else (early.chunk, cells)
    big, small = iota(shape, 1 if down else 0), iota(shape, 0 if down else 1)
    same_line = big // (2 * early.stride) == small // late.stride
    return ones_where(same_line & (big % early.stride // 2 == small % late.stride))


def token_matrix(late, starts, first, rows, down):
    shape = (rows, late.rows) if down else (late.chunk, rows)
    packed, cell = iota(shape, 0 if down else 1), iota(shape, 1 if down else 0)
    if down:
        packed += first
    else:
        cell += first
    inside = cell % (late.side * late.stride)
    line, column = inside // late.stride, inside % late.stride
    image = cell // (late.side * late.stride)
    start = jnp.zeros(shape, jnp.int32)
    for n in range(late.images):
        start = jnp.where(image == n, starts[n], start)
    return ones_where((packed == start + line * late.side + column) & (column < late.side))


PIECES = 16
RING = 8
RING_LINES = 4


class Plan:
    def __init__(self, images, side, channels, width, group, ring, hidden, out):
        self.early, self.late = Grid(images, side, width), Grid(images, side // 2, width)
        self.images, self.channels, self.width, self.out = images, channels, width, out
        self.span = (side // 2) ** 2
        self.block = images * self.span
        self.group, self.chips = group, group // 2
        self.rows = group * self.block
        self.ring = ring == RING and group == 4
        self.hidden = hidden
        self.piece = out // PIECES
        self.slab = channels // PIECES
        taps = 9 * width
        self.kernel_at = (0, taps)
        self.reduce_at = (2 * taps, 2 * taps + channels)
        self.expand_at = (2 * taps + 2 * channels, 2 * taps + 3 * channels)
        self.small_at = 2 * taps + 4 * channels
        self.small_block = 4 + 2 * channels // width
        self.small = 2 * self.small_block + out // width + group * hidden // width
        self.flat_piece = -(-(self.small_at + self.small) // (group * PIECES * 16)) * 16
        self.flat = group * PIECES * self.flat_piece


def ring_place(device):
    line, column = device // 2, lax.rem(device, 2)
    return (1 - column) * line + column * (2 * RING_LINES - 1 - line)


def ring_device(place):
    column = place // RING_LINES
    return 2 * ((1 - column) * place + column * (2 * RING_LINES - 1 - place)) + column


class Ring:
    def __init__(self, place, held, first, out, sems, local, window, tap=None):
        self.place, self.held, self.first, self.out = place, held, first, out
        self.sems, self.local, self.window, self.tap = sems, local, window, tap
        ahead = ring_device(lax.rem(place + 1, RING))
        behind = ring_device(lax.rem(place + RING - 1, RING))
        self.to = (ahead, behind)

    def index(self, way, step):
        turn = self.place - step if way == 0 else self.place + step
        return way * RING + lax.rem(turn + 2 * RING, RING)

    def landed(self, index):
        return self.out.at[index, self.window, :]

    def copy(self, way, step, gather):
        if gather:
            target = self.landed(self.index(way, step - 1))
            source = self.held.at[way, RING - 2, self.window, :] if step == 0 else target
        else:
            source = self.first.at[way, self.window, :]
            if step:
                source = self.held.at[way, step - 1, self.window, :]
            target = self.held.at[way, step, self.window, :]
        return pltpu.make_async_remote_copy(
            src_ref=source,
            dst_ref=target,
            send_sem=self.sems[2 * gather].at[way, step],
            recv_sem=self.sems[2 * gather + 1].at[way, step],
            device_id={"dp": self.to[way]},
            device_id_type=MESH,
        )

    def keep(self, way):
        source = self.held.at[way, RING - 2, self.window, :]
        return pltpu.make_async_copy(source, self.landed(self.index(way, -1)), self.local.at[way])

    def reduce(self, step, partial):
        for way in range(2):
            if step:
                self.copy(way, step - 1, 0).wait_recv()
            target = self.first.at[way] if step == 0 else self.held.at[way, step - 1]

            def put(window, value, target=target):
                if step:
                    value = value + target[window].astype(f32)
                target[window] = value.astype(bf16)

            partial(way, self.index(way, step), put)
            if step < RING - 1:
                self.copy(way, step, 0).start()
            else:
                self.copy(way, 0, 1).start()
                self.keep(way).start()
                if self.tap:
                    self.tap(way, 0, self.index(way, -1), self.held.at[way, RING - 2, self.window, :])

    def gather(self, step):
        for way in range(2):
            self.copy(way, step - 1, 1).wait_recv()
            index = self.index(way, step - 1)
            if step < RING - 1:
                self.copy(way, step, 1).start()
            if self.tap:
                self.tap(way, step, index, self.landed(index))

    def tick(self, count, partial):
        if count < RING:
            self.reduce(count, partial)
        else:
            self.gather(count - RING + 1)

    def finish(self):
        for way in range(2):
            self.keep(way).wait()
            for step in range(RING - 1):
                self.copy(way, step, 0).wait_send()
                self.copy(way, step, 1).wait_send()


TICKS = 2 * RING - 1
SUBS = 2


def mega(plan, names, *all_refs):
    r = dict(zip(names, all_refs))
    early, late, block, chips, group = plan.early, plan.late, plan.block, plan.chips, plan.group
    hid, out, piece, ch, width = plan.hidden, plan.out, plan.piece, plan.channels, plan.width
    me = lax.axis_index("tensor")
    chip, core = me // 2, lax.rem(me, 2)
    place = ring_place(lax.axis_index("dp")) if plan.ring else 0 * me
    pair = {"tensor": 2 * chip + 1 - core}
    ep, lp = ([r[f"{name}{k}"] for k in range(9)] for name in ("early", "late"))

    def other(hop):
        return {"tensor": 2 * lax.rem(chip + hop + chips, chips) + core}

    started = []

    def send(source, target, name, at, device):
        return pltpu.make_async_remote_copy(
            src_ref=source,
            dst_ref=target,
            send_sem=r[name + "_s"].at[at],
            recv_sem=r[name + "_r"].at[at],
            device_id=device,
            device_id_type=MESH,
        )

    def go(copy, keep=True):
        copy.start()
        if keep:
            started.append(copy)

    def order(step):
        back, forth = lax.rem(place - step + 2 * RING, RING), lax.rem(place + step, RING)
        return (back, RING + forth)

    def columns(index, size):
        return pl.ds(pl.multiple_of(index * size, 128), size)

    def rows_at(index, size):
        return pl.ds(pl.multiple_of(index * size, 16), size)

    sems = [r[f"ring_{kind}"] for kind in ("rs", "rr", "gs", "gr")]

    def ring_of(n, held, first, target, window, tap=None):
        mine = [sem.at[n] for sem in sems]
        return Ring(place, held, first, target, mine, r["ring_l"].at[n], window, tap)

    gflat = r["gflat"]

    def to_pair(hop, way, step, index, source):
        target = gflat.at[core, lax.rem(chip - hop + chips, chips), index]
        return send(source, target, "ac", (hop, way, step), pair)

    def spread_piece(way, step, index, source):
        for hop in range(1, chips):
            go(send(source, gflat.at[core, chip, index], "ax", (hop - 1, way, step), other(hop)))
        go(to_pair(0, way, step, index, source))

    part_rows = hid // SUBS
    one = [
        ring_of(k, r["held"], r["first"], r["gout"], pl.ds(k * part_rows, part_rows)) for k in range(SUBS)
    ]
    two = ring_of(SUBS, r["held2"], r["first2"], r["gin"], pl.ds(0, plan.slab))
    three = None
    if plan.ring:
        whole = pl.ds(0, plan.flat_piece)
        three = ring_of(SUBS + 1, r["held3"], r["first3"], gflat.at[core, chip], whole, spread_piece)

    barrier = pltpu.get_barrier_semaphore()
    friends = [pair] + [other(hop) for hop in range(1, chips)]
    if plan.ring:
        friends += [{"dp": two.to[0]}, {"dp": two.to[1]}]
    for friend in friends:
        pl.semaphore_signal(barrier, inc=1, device_id=friend, device_id_type=MESH)
    pl.semaphore_wait(barrier, len(friends))

    cot, gall = r["cot"], r["gall"]

    def cot_own(step):
        for way, index in enumerate(order(step)):
            go(send(cot.at[:, columns(index, piece)], gall.at[1, index], "cc", (0, step, way), pair))

    def cot_far(step):
        for hop in range(1, chips):
            for way, index in enumerate(order(step)):
                source = cot.at[:, columns(index, piece)]
                go(send(source, gall.at[2 * hop, index], "cx", (hop - 1, step, way), other(hop)))

    def cot_pass(step):
        for hop in range(1, chips):
            for way, index in enumerate(order(step)):
                source = gall.at[2 * hop, index]
                send(source, source, "cx", (hop - 1, step, way), other(hop)).wait_recv()
                go(send(source, gall.at[2 * hop + 1, index], "cc", (hop, step, way), pair))

    ready = set()

    def cot_ready(step):
        if step in ready:
            return
        ready.add(step)
        for hop in range(chips):
            for way, index in enumerate(order(step)):
                target = gall.at[2 * hop + 1, index]
                send(target, target, "cc", (hop, step, way), pair).wait_recv()

    fetch = pltpu.make_async_copy(r["x"], r["xs"], r["load"].at[0])
    fetch.start()
    for step in range(3):
        cot_far(step)
    for step in range(RING):
        cot_own(step)
    fetch.wait()

    xs, pool, act, tok, big = r["xs"], r["pool"], r["act"], r["tok"], r["big"]
    cells = early.lines // 2 * late.stride

    def load_early(i):
        return xs[early.here(i), :]

    def load_late(i):
        return pool[late.here(i), :]

    def put_early(i, value):
        pool[rows_at(i, cells), :] = two_part(pool_matrix(early, late, True), value) * 0.25

    tsend, tpair, tfar = r["tsend"], r["tpair"], r["tfar"]

    def put_late(i, value):
        tsend[i, 0 : late.chunk, :] = value.astype(bf16)

    block_forward(early, load_early, ep, r["ered"], r["econv"], big, put_early)
    block_forward(late, load_late, lp, r["lred"], r["lconv"], big, put_late)
    for n in range(plan.images):
        matrix = token_matrix(late, r["starts"], n * plan.span, plan.span, True)
        value = None
        for i in range(late.chunks):
            part = dot(matrix[:, i * late.chunk : (i + 1) * late.chunk], tsend[i, 0 : late.chunk, :])
            value = part if value is None else value + part
        tok[0, n * plan.span : (n + 1) * plan.span, :] = value.astype(bf16)
    token_sends = [send(tok.at[0], tok.at[2 * hop], "tx", (hop - 1,), other(hop)) for hop in range(1, chips)]
    token_sends.append(send(tok.at[0], tok.at[1], "tc", (0,), pair))
    for copy in token_sends:
        copy.start()
    for step in range(3, RING):
        cot_far(step)
    for step in range(3):
        cot_pass(step)

    slope, win = r["slope"], r["win"]

    def hidden_of(j):
        half = block // 2

        def body(i, _):
            pre = dot(tok[j, rows_at(i, half), :], win[...]) + r["bin"][...].astype(f32)
            bend = jnp.tanh(0.7978845608 * (pre + 0.044715 * pre * pre * pre))
            rows = rows_at(2 * j + i, half)
            act[rows, :] = (0.5 * pre * (1.0 + bend)).astype(bf16)
            rise = 0.7978845608 * (1.0 + 3.0 * 0.044715 * pre * pre)
            slope[rows, :] = (0.5 * (1.0 + bend) + 0.5 * pre * (1.0 - bend * bend) * rise).astype(bf16)
            return 0

        lax.fori_loop(0, 2, body, 0)

    hidden_of(0)
    send(tok.at[0], tok.at[1], "tc", (0,), pair).wait_recv()
    hidden_of(1)
    for hop in range(1, chips):
        send(tok.at[0], tok.at[2 * hop], "tx", (hop - 1,), other(hop)).wait_recv()
        token_sends.append(send(tok.at[2 * hop], tok.at[2 * hop + 1], "tc", (hop,), pair))
        token_sends[-1].start()
        hidden_of(2 * hop)
        send(tok.at[0], tok.at[2 * hop + 1], "tc", (hop,), pair).wait_recv()
        hidden_of(2 * hop + 1)

    turned, gbuf = r["turned"], r["gbuf"]

    def turn(i, _):
        stripe = act[:, columns(i, 128)].astype(f32)
        turned[rows_at(i, 128), :] = jnp.transpose(stripe).astype(bf16)
        return 0

    lax.fori_loop(0, hid // 128, turn, 0)

    def cot_piece(j, index):
        return cot.at[:, columns(index, piece)] if j == 0 else gall.at[j, index]

    def piece_loads(step, way):
        slot, index = step % 2, order(step)[way]
        loads = []
        for j in range(group):
            target = gbuf.at[slot, way, pl.ds(j * block, block), :]
            loads.append(pltpu.make_async_copy(cot_piece(j, index), target, r["gload"].at[slot, way, j]))
        return loads

    def prepare(step):
        cot_ready(step)
        for way in range(2):
            for load in piece_loads(step, way):
                load.start()

    def piece_of(step, sub):
        def partial(way, index, put):
            tile = gbuf.at[step % 2, way]
            if sub == 0:
                for load in piece_loads(step, way):
                    load.wait()

            def body(i, _):
                rows = pl.ds(pl.multiple_of(sub * part_rows + i * 256, 256), 256)
                put((rows, slice(None)), dot(turned[rows, :], tile[...]))
                return 0

            lax.fori_loop(0, part_rows // 256, body, 0)

        return partial

    def alone(step, ring, partial):
        for way, index in enumerate(order(step)):
            stage = ring.first.at[way]

            def put(window, value, stage=stage):
                stage[window] = value.astype(bf16)

            partial(way, index, put)
            write = pltpu.make_async_copy(stage.at[ring.window, :], ring.landed(index), ring.local.at[way])
            write.start()
            write.wait()

    def tick(ring, count, partial):
        if plan.ring:
            ring.tick(count, partial)
        elif count < RING:
            alone(count, ring, partial)

    def tick_one(count):
        step, sub = count // SUBS, count % SUBS
        tick(one[sub], step, piece_of(step, sub))
        if sub == 0 and step + 1 < RING:
            prepare(step + 1)

    wout, wbuf, rbuf = r["wout"], r["wbuf"], r["rbuf"]
    tiles = out // piece

    def result_pass(blocks, extra, finish, low, high):
        def loads(i, slot):
            cols = columns(i, piece)
            pairs = [(wout.at[:, cols], wbuf.at[slot])]
            for n, ref in enumerate(extra):
                pairs.append((ref.at[:, cols], turned.at[pl.ds(n * block, block), columns(slot, piece)]))
            return [pltpu.make_async_copy(a, b, r["wload"].at[slot, n]) for n, (a, b) in enumerate(pairs)]

        for k in range(3):
            for load in loads(low + k, k):
                load.start()

        def body(k, _):
            i, slot = low + k, lax.rem(k, 4)
            for load in loads(i, slot):
                load.wait()

            @pl.when(i + 3 < high)
            def _():
                for load in loads(i + 3, lax.rem(k + 3, 4)):
                    load.start()

            for n, j in enumerate(blocks):
                value = dot(act[j * block : (j + 1) * block, :], wbuf[slot])
                for m in range(len(extra)):
                    value += turned[m * block : (m + 1) * block, columns(slot, piece)].astype(f32)
                finish(n, i, value)
            return 0

        lax.fori_loop(0, high - low, body, 0)

    def pair_copy(hop):
        return send(rbuf.at[hop], r["rpair"].at[hop], "rp", (hop,), pair)

    def result_pairs(low, high):
        def put(n, i, value):
            rbuf[n, :, columns(i, piece)] = value.astype(bf16)

        result_pass([2 * hop + 1 for hop in range(chips)], [], put, low, high)
        if high == tiles:
            for hop in range(chips):
                go(pair_copy(hop), False)

    def result_pairs_done():
        for hop in range(chips):
            pair_copy(hop).wait()

    def result_far():
        for hop in range(chips - 1, 0, -1):
            extra = [r["rpair"].at[hop]]
            if hop < chips - 1:
                send(rbuf.at[0], r["rfar"].at[hop], "rx", (hop,), other(-1)).wait_recv()
                extra.append(r["rfar"].at[hop])

            def put(n, i, value, hop=hop):
                rbuf[hop, :, columns(i, piece)] = value.astype(bf16)

            result_pass([2 * hop], extra, put, 0, tiles)
            go(send(rbuf.at[hop], r["rfar"].at[hop - 1], "rx", (hop - 1,), other(-1)))

    def result_own():
        send(rbuf.at[0], r["rfar"].at[0], "rx", (0,), other(-1)).wait_recv()

        def put(n, i, value):
            cols = columns(i, piece)
            rbuf[0, :, cols] = (value + r["bout"][:, cols].astype(f32)).astype(bf16)

        result_pass([0], [r["rpair"].at[0], r["rfar"].at[0]], put, 0, tiles)
        go(pltpu.make_async_copy(rbuf.at[0], r["projected"], r["load"].at[1]))

    flat = r["flat"]
    rows_all = plan.rows

    def active_rows(slot, way, j):
        return rows_at(2 * slot + way, rows_all) if j is None else pl.ds(
            pl.multiple_of((2 * slot + way) * rows_all + j * block, 16), block
        )

    def active_loads(step, slot):
        loads = []
        for way, index in enumerate(order(step)):
            for j in range(group):
                target = flat.at[active_rows(slot, way, j), :]
                sem = r["aload"].at[slot, way, j]
                loads.append(pltpu.make_async_copy(cot_piece(j, index), target, sem))
            sem = r["aload"].at[slot, way, group]
            target = wbuf.at[2 * slot + way]
            loads.append(pltpu.make_async_copy(wout.at[:, columns(index, piece)], target, sem))
        return loads

    def active_steps(low, high):
        if low == 0:
            for load in active_loads(0, 0):
                load.start()

        def body(step, _):
            slot = lax.rem(step, 2)
            for load in active_loads(step, slot):
                load.wait()

            @pl.when(step + 1 < RING)
            def _():
                for load in active_loads(step + 1, 1 - slot):
                    load.start()

            for way, index in enumerate(order(step)):
                own = flat[active_rows(slot, way, 0), :].astype(f32)
                r["outbias"][pl.ds(index, 1), :] = column_sum(own)

            def rows_of(j, _):
                rows = rows_at(j, block)
                value = dot_nt(flat[active_rows(slot, 0, j), :], wbuf[2 * slot])
                value += dot_nt(flat[active_rows(slot, 1, j), :], wbuf[2 * slot + 1])
                before = big[rows, 0:hid]
                big[rows, 0:hid] = value + (jnp.where(step == 0, 0.0, before) if low == 0 else before)
                return 0

            lax.fori_loop(0, group, rows_of, 0)
            return 0

        lax.fori_loop(low, high, body, 0)

    def hidden_back():
        r["inbias"][...] = jnp.zeros(r["inbias"].shape, f32)

        def body(i, _):
            rows = rows_at(i, block // 2)
            value = (big[rows, 0:hid] * slope[rows, :].astype(f32)).astype(bf16)
            slope[rows, :] = value
            r["inbias"][...] += column_sum(value.astype(f32))
            return 0

        lax.fori_loop(0, 2 * group, body, 0)

    def tokens_back(j):
        return dot_nt(slope[j * block : (j + 1) * block, :], win[...])

    def tokens_pair(hop):
        return send(tsend.at[hop], tpair.at[hop], "gc", (hop,), pair)

    def tokens_far_copy(hop):
        return send(tsend.at[hop], tfar.at[hop - 1], "gx_", (hop - 1,), other(-1))

    def fetched(source, target):
        load = pltpu.make_async_copy(source, target, r["load"].at[2])
        load.start()
        load.wait()
        return target[...].astype(f32)

    def tokens_far():
        for hop in range(chips - 1, -1, -1):
            tsend[hop] = tokens_back(2 * hop + 1).astype(bf16)
            go(tokens_pair(hop), False)
        for hop in range(chips - 1, 0, -1):
            value = tokens_back(2 * hop)
            tokens_pair(hop).wait()
            value = value + fetched(tpair.at[hop], tsend.at[hop])
            if hop < chips - 1:
                tokens_far_copy(hop + 1).wait_recv()
                value = value + fetched(tfar.at[hop], tsend.at[hop])
            tsend[hop] = value.astype(bf16)
            go(tokens_far_copy(hop))

    def tokens_own():
        value = tokens_back(0)
        tokens_pair(0).wait()
        value = value + fetched(tpair.at[0], tsend.at[0])
        tokens_far_copy(1).wait_recv()
        value = value + fetched(tfar.at[0], tsend.at[0])
        high = value.astype(bf16)
        tsend[0] = high
        rest = (value - high.astype(f32)).astype(bf16)
        for i in range(late.chunks):
            matrix = token_matrix(late, r["starts"], i * late.chunk, block, False)
            r["gpool"][i * late.chunk : (i + 1) * late.chunk, :] = dot(matrix, tsend[0]) + dot(matrix, rest)

    parts = hid // 256

    def weights_in():
        for copy in token_sends:
            copy.wait_send()

        def body(i, _):
            total = None
            for j in range(group):
                part = dot_tn(tok[j, :, columns(i, 256)], slope[j * block : (j + 1) * block, :])
                total = part if total is None else total + part
            for q in range(parts):
                tok[q, 0:256, columns(i, 256)] = total[:, q * 256 : (q + 1) * 256].astype(bf16)
            return 0

        lax.fori_loop(0, ch // 256, body, 0)

    def slab_of(way, index, put):
        each = 256 // plan.slab
        for q in range(parts):
            value = tok[q, rows_at(lax.rem(index, each), plan.slab), columns(index // each, 256)]
            put((slice(None), slice(q * 256, (q + 1) * 256)), value.astype(f32))

    def tick_two(count):
        tick(two, count, slab_of)

    gpool = r["gpool"]
    acc = [r[f"acc{k}"] for k in range(9)]

    def late_back():
        def put(i, value):
            gpool[late.here(i), :] = value * 0.25

        def grad(i):
            return gpool[late.here(i), :]

        cuts = [[(0, late.chunks)]] * 2
        return block_backward(late, load_late, grad, lp, r["lred"], r["lconv"], big, acc, put, cuts)

    def early_back():
        def grad(i):
            return two_part(pool_matrix(early, late, False), gpool[rows_at(i, cells), :])

        def put(i, value):
            xs[early.here(i), :] = value.astype(bf16)

        count = early.chunks
        cuts = [[(0, count // 2), (count // 2, count)]]
        cuts.append([(k * count // 3, (k + 1) * count // 3) for k in range(3)])
        return block_backward(early, load_early, grad, ep, r["ered"], r["econv"], big, acc, put, cuts)

    small = r["small"]

    def store_flat(n):
        flat[pl.ds(plan.kernel_at[n], 9 * width), :] = acc[3][...].astype(bf16)
        flat[pl.ds(plan.reduce_at[n], ch), :] = acc[0][...].astype(bf16)
        quarters = ch // width
        for q in range(quarters):
            rows = pl.ds(plan.expand_at[n] + q * width, width)
            flat[rows, :] = acc[6][:, q * width : (q + 1) * width].astype(bf16)
        at = n * plan.small_block
        for k, ref in enumerate((acc[1], acc[2], acc[4], acc[5])):
            small[at + k : at + k + 1, :] = ref[...]
        for k, ref in enumerate((acc[7], acc[8])):
            for q in range(quarters):
                row = at + 4 + k * quarters + q
                small[row : row + 1, :] = ref[:, q * width : (q + 1) * width]

    def store_small():
        at = 2 * plan.small_block
        small[at : at + out // width, :] = r["outbias"][...]
        at += out // width
        for owner in range(group):
            for q in range(hid // width):
                row = at + owner * (hid // width) + q
                part = r["inbias"][:, q * width : (q + 1) * width]
                small[row : row + 1, :] = jnp.where(me == owner, part, 0.0)
        row = at + group * hid // width
        small[row:, :] = jnp.zeros((small.shape[0] - row, width), f32)
        flat[pl.ds(plan.small_at, small.shape[0]), :] = small[...].astype(bf16)
        rest = plan.small_at + small.shape[0]
        flat[pl.ds(rest, plan.flat - rest), :] = jnp.zeros((plan.flat - rest, width), bf16)

    half, quarter = plan.flat // 2, plan.flat // group
    flat_piece = plan.flat_piece

    def flat_pair():
        away = flat.at[rows_at(1 - core, half), :]
        return send(away, r["fpair"], "fp", (0,), pair)

    def flat_far_copy(hop):
        return send(gbuf.at[1], r["ffar"], "fx", (hop - 1,), other(hop))

    def own_piece(index):
        across = big.shape[1] // width
        return rows_at(index // across, flat_piece), columns(lax.rem(index, across), width)

    upper = PIECES // 2

    def stage(sources):
        loads = [
            pltpu.make_async_copy(source, gbuf.at[0, n], r["load"].at[2 + n])
            for n, source in enumerate(sources)
        ]
        for load in loads:
            load.start()
        for load in loads:
            load.wait()

    def staged(i):
        return (i // upper, rows_at(lax.rem(i, upper), flat_piece))

    def flat_far():
        flat_pair().wait_recv()
        for hop in range(chips - 1, -1, -1):
            to = lax.rem(chip + hop, chips)
            stage([r["fpair"].at[rows_at(2 * to + n, quarter // 2), :] for n in range(2)])

            def body(i, _, hop=hop, to=to):
                mine = pl.ds(pl.multiple_of(core * half + to * quarter + i * flat_piece, 16), flat_piece)
                total = flat[mine, :].astype(f32) + gbuf[(0, *staged(i))].astype(f32)
                if hop:
                    gbuf[(1, *staged(i))] = total.astype(bf16)
                else:
                    big[own_piece(i)] = total
                return 0

            lax.fori_loop(0, PIECES, body, 0)
            if hop:
                go(flat_far_copy(hop))

    def flat_sum():
        for hop in range(1, chips):
            flat_far_copy(hop).wait_recv()
            stage([r["ffar"].at[n] for n in range(2)])

            def body(i, _):
                big[own_piece(i)] += gbuf[(0, *staged(i))].astype(f32)
                return 0

            lax.fori_loop(0, PIECES, body, 0)

    def flat_of(way, index, put):
        put((slice(None), slice(None)), big[own_piece(index)])

    def tick_three(count):
        tick(three, count, flat_of)

    def flat_spread():
        for hop in range(1, chips):
            theirs = gflat.at[core, lax.rem(chip - hop + chips, chips)]
            for step in range(RING):
                for way in range(2):
                    index = three.index(way, step - 1)
                    ref = theirs.at[index]
                    send(ref, ref, "ax", (hop - 1, way, step), other(hop)).wait_recv()
                    go(to_pair(hop, way, step, index, ref))
        for hop in range(chips):
            for step in range(RING):
                for way in range(2):
                    index = three.index(way, step - 1)
                    to_pair(hop, way, step, index, gflat.at[core, 0, index]).wait_recv()

    def early_ready(low, high):
        for step in range(low, high):
            cot_ready(step)

    prepare(0)
    tick_one(0)
    tick_one(1)
    early_ready(0, 3)
    active_steps(0, 2)
    cot_pass(3)
    cot_pass(4)
    tick_one(2)
    early_ready(0, 4)
    active_steps(2, 3)
    cot_pass(5)
    tick_one(3)
    early_ready(0, 6)
    active_steps(3, 5)
    tick_one(4)
    cot_pass(6)
    early_ready(0, 7)
    active_steps(5, 6)
    tick_one(5)
    cot_pass(7)
    early_ready(0, RING)
    active_steps(6, RING)
    tick_one(6)
    hidden_back()
    tokens_far()
    tick_one(7)
    weights_in()
    tick_one(8)
    result_pairs(0, tiles // 2)
    tick_one(9)
    tokens_own()
    tick_two(0)
    part = late_back()
    next(part)
    tick_one(10)
    next(part)
    store_flat(1)
    tick_one(11)
    part = early_back()
    next(part)
    tick_two(1)
    tick_one(12)
    next(part)
    tick_one(13)
    next(part)
    tick_two(2)
    tick_one(14)
    next(part)
    tick_one(15)
    next(part)
    go(pltpu.make_async_copy(xs, r["gx"], r["load"].at[0]))
    store_flat(0)
    store_small()
    if plan.ring:
        go(flat_pair())
    else:
        go(pltpu.make_async_copy(flat, gflat, r["load"].at[2]))
    tick_two(3)
    tick_one(16)
    if plan.ring:
        flat_far()
    tick_one(17)
    result_pairs(tiles // 2, tiles)
    tick_two(4)
    tick_one(18)
    result_pairs_done()
    result_far()
    tick_two(5)
    later = 0
    for count in range(19, SUBS * TICKS):
        tick_one(count)
        if count - 13 < TICKS:
            tick_two(count - 13)
        if plan.ring and count == 19:
            flat_sum()
        for _ in range(1 + count % 2 if plan.ring else 0):
            if later < TICKS:
                tick_three(later)
                later += 1
        if count == SUBS * TICKS - 4:
            result_own()
    if plan.ring:
        while later < TICKS:
            tick_three(later)
            later += 1
        three.finish()
        flat_spread()
        for ring in (*one, two):
            ring.finish()
    for copy in started:
        if copy.is_remote:
            copy.wait_send()
        else:
            copy.wait()


def unpack_body(group, gout, gin, gx, kernel0, kernel1, reduce0, reduce1, expand0, expand1, small, *outs):
    big_outs, small_outs = outs[:9], outs[9:]
    size = gout.shape[2]
    for piece in range(PIECES):
        big_outs[0][:, piece * size : (piece + 1) * size] = gout[piece].astype(f32)
    big_outs[1][...] = gin[0].astype(f32)
    for source, target in zip((gx, kernel0, kernel1, reduce0, reduce1, expand0, expand1), big_outs[2:]):
        target[...] = source[...].astype(f32)

    @pl.when(pl.program_id(0) == 0)
    def _():
        row, width = 0, small.shape[1]
        last = small_outs[-1]
        parts = last.shape[1] // width
        me = lax.axis_index("tensor")
        for target in small_outs[:-1]:
            for q in range(target.shape[1] // width):
                target[:, q * width : (q + 1) * width] = small[row : row + 1, :].astype(f32)
                row += 1
        for q in range(parts):
            value = None
            for owner in range(group):
                at = row + owner * parts + q
                mine = jnp.where(me == owner, small[at : at + 1, :].astype(f32), 0.0)
                value = mine if value is None else value + mine
            last[:, q * width : (q + 1) * width] = value


def unpack(plan, gout, gin, gx, flat):
    width, ch, hid, out, group = plan.width, plan.channels, plan.hidden, plan.out, plan.group
    shape = partial(jax.ShapeDtypeStruct, dtype=f32)
    taps, steps = 9 * width, PIECES
    quarters = ch // width
    each = steps // quarters

    def rows_spec(size, start, columns=width):
        assert start % size == 0
        return pl.BlockSpec((size, columns), lambda i: (start // size + i, 0))

    lane = width // each
    in_specs = [
        pl.BlockSpec((PIECES, hid // steps, plan.piece), lambda i: (0, i, 0)),
        pl.BlockSpec((1, plan.slab, hid), lambda i: (i, 0, 0)),
        rows_spec(plan.early.rows // steps, 0, ch),
        *[rows_spec(taps // steps, plan.kernel_at[n]) for n in range(2)],
        *[rows_spec(ch // steps, plan.reduce_at[n]) for n in range(2)],
        *[rows_spec(lane, plan.expand_at[n]) for n in range(2)],
        pl.BlockSpec((128, width), lambda i: (plan.small_at // 128, 0)),
    ]
    expand_out = pl.BlockSpec((lane, width), lambda i: (i % each, i // each))
    smalls = [width] * 4 + [ch] * 2
    smalls = smalls + smalls + [out, hid]
    out_specs = [
        rows_spec(hid // steps, 0, out),
        rows_spec(plan.slab, 0, hid),
        rows_spec(plan.early.rows // steps, 0, ch),
        *[rows_spec(taps // steps, 0)] * 2,
        *[rows_spec(ch // steps, 0)] * 2,
        *[expand_out] * 2,
        *[pl.BlockSpec((1, size), lambda i: (0, 0)) for size in smalls],
    ]
    out_shape = [shape((hid, out)), shape((ch, hid)), shape((plan.early.rows, ch))]
    out_shape += [shape((taps, width))] * 2 + [shape((ch, width))] * 2 + [shape((width, ch))] * 2
    out_shape += [shape((1, size)) for size in smalls]
    return pl.pallas_call(
        partial(unpack_body, group), grid=(steps,), in_specs=in_specs, out_specs=out_specs, out_shape=out_shape
    )(gout, gin, gx, *[flat] * 7)


def shards(*args):
    patches, early, late = args[0], args[1:10], args[10:19]
    readin_weight, readin_bias, readout_weight, readout_bias, cotangent, span_start = args[19:]
    images, side, _, channels = patches.shape
    width, hidden, out = early[0].shape[1], readin_weight.shape[1], readout_weight.shape[1]
    group, ring = lax.axis_size("tensor"), lax.axis_size("dp")
    plan = Plan(images, side, channels, width, group, ring, hidden, out)
    chips, block, rows = plan.chips, plan.block, plan.rows

    def matrices(params):
        kernel = params[3].reshape(3, 3 * width, width)
        return [params[0], params[1][None], params[2][None], kernel, params[4][None], params[5][None],
                params[6], params[7][None], params[8][None]]

    inputs = {"starts": span_start, "x": patches.reshape(-1, channels)}
    inputs |= {f"early{k}": item for k, item in enumerate(matrices(early))}
    inputs |= {f"late{k}": item for k, item in enumerate(matrices(late))}
    inputs |= {"win": readin_weight, "bin": readin_bias[None], "wout": readout_weight,
               "bout": readout_bias[None], "cot": cotangent}
    quarter = plan.flat // group
    gflat = (2, chips, PIECES, plan.flat_piece, width) if plan.ring else (plan.flat, width)
    outputs = {
        "projected": (block, out),
        "gx": (plan.early.rows, channels),
        "gout": (PIECES, hidden, plan.piece),
        "gin": (PIECES, plan.slab, hidden),
        "gflat": gflat,
        "gall": (group, PIECES, block, plan.piece),
        "rpair": (chips, block, out),
        "rfar": (max(chips - 1, 1), block, out),
        "tpair": (chips, block, channels),
        "tfar": (chips - 1, block, channels),
        "fpair": (plan.flat // 2, width),
        "ffar": (2, quarter // 2, width),
    }
    hops = RING - 1
    early_rows, late_rows = plan.early.rows, plan.late.rows
    low = {
        "xs": (early_rows, channels),
        "tok": (group, block, channels),
        "act": (rows, hidden),
        "slope": (rows, hidden),
        "turned": (max(hidden, 2 * block), rows),
        "gbuf": (2, 2, rows, plan.piece),
        "held": (2, hops, hidden, plan.piece),
        "first": (2, hidden, plan.piece),
        "wbuf": (4, hidden, plan.piece),
        "rbuf": (chips, block, out),
        "tsend": (chips, block, channels),
        "held2": (2, hops, plan.slab, hidden),
        "first2": (2, plan.slab, hidden),
        "held3": (2, hops, plan.flat_piece, width),
        "first3": (2, plan.flat_piece, width),
        "flat": (plan.flat, width),
    }
    wide = {
        "pool": (late_rows, channels),
        "gpool": (late_rows, channels),
        "ered": (early_rows, width),
        "econv": (early_rows, width),
        "lred": (late_rows, width),
        "lconv": (late_rows, width),
        "big": (max(plan.early.padded, rows), max(3 * width, hidden)),
        "small": (64, width),
        "outbias": (PIECES, plan.piece),
        "inbias": (1, hidden),
        "acc0": (channels, width),
        "acc1": (1, width),
        "acc2": (1, width),
        "acc3": (9 * width, width),
        "acc4": (1, width),
        "acc5": (1, width),
        "acc6": (width, channels),
        "acc7": (1, channels),
        "acc8": (1, channels),
    }
    remote = {
        "cx": (chips - 1, RING, 2),
        "cc": (chips, RING, 2),
        "tx": (chips - 1,),
        "tc": (chips,),
        "rp": (chips,),
        "rx": (chips - 1,),
        "gc": (chips,),
        "gx_": (chips - 1,),
        "fp": (1,),
        "fx": (chips - 1,),
        "ax": (chips - 1, 2, RING),
        "ac": (chips, 2, RING),
    }
    copies = {f"{name}_{end}": size for name, size in remote.items() for end in "sr"}
    copies |= {f"ring_{kind}": (SUBS + 2, 2, hops) for kind in ("rs", "rr", "gs", "gr")}
    copies |= {"ring_l": (SUBS + 2, 2), "load": (4,), "gload": (2, 2, group), "wload": (4, 3), "aload": (2, 2, group + 1)}
    hbm, vmem = pl.BlockSpec(memory_space=pltpu.HBM), pl.BlockSpec(memory_space=pltpu.VMEM)
    kinds = {"starts": pl.BlockSpec(memory_space=pltpu.SMEM), "x": hbm, "wout": hbm, "cot": hbm}
    scratch = [pltpu.VMEM(size, bf16) for size in low.values()]
    scratch += [pltpu.VMEM(size, f32) for size in wide.values()]
    scratch += [pltpu.SemaphoreType.DMA(size) for size in copies.values()]
    names = [*inputs, *outputs, *low, *wide, *copies]
    landed = pl.pallas_call(
        partial(mega, plan, names),
        out_shape=[jax.ShapeDtypeStruct(size, bf16) for size in outputs.values()],
        in_specs=[kinds.get(name, vmem) for name in inputs],
        out_specs=[hbm] * len(outputs),
        scratch_shapes=scratch,
        compiler_params=pltpu.CompilerParams(
            collective_id=0, has_side_effects=True, vmem_limit_bytes=67043328
        ),
    )(*inputs.values())
    projected, grad_x, gout, gin, flat = landed[:5]
    flat = flat.reshape(plan.flat, width)
    if not plan.ring:
        gout, gin = lax.psum(gout, "dp"), lax.psum(gin, "dp")
        flat = lax.psum(flat, ("dp", "tensor"))
    done = unpack(plan, gout, gin, grad_x, flat)
    grad_readout, grad_readin, grad_patches = done[:3]
    kernels, reduces, expands, smalls = done[3:5], done[5:7], done[7:9], done[9:]

    def grads(n):
        small = [item.reshape(-1) for item in smalls[6 * n : 6 * n + 6]]
        kernel = kernels[n].reshape(3, 3, width, width)
        return [reduces[n], small[0], small[1], kernel, small[2], small[3], expands[n], small[4], small[5]]

    return (
        projected,
        grad_patches.reshape(patches.shape),
        *grads(0),
        *grads(1),
        grad_readin,
        smalls[13].reshape(-1),
        grad_readout,
        smalls[12].reshape(-1),
    )


def solution(mesh):
    in_specs = (
        P(("dp", "tensor"), None, None, None),
        P(),
        P(),
        P(),
        P(),
        P(),
        P(),
        P(),
        P(),
        P(),
        P(),
        P(),
        P(),
        P(),
        P(),
        P(),
        P(),
        P(),
        P(),
        P(None, "tensor"),
        P("tensor"),
        P("tensor", None),
        P(),
        P(("dp", "tensor"), None),
        P(("dp", "tensor")),
    )
    out_specs = (
        P(("dp", "tensor"), None),
        P(("dp", "tensor"), None, None, None),
        P(),
        P(),
        P(),
        P(),
        P(),
        P(),
        P(),
        P(),
        P(),
        P(),
        P(),
        P(),
        P(),
        P(),
        P(),
        P(),
        P(),
        P(),
        P(None, "tensor"),
        P("tensor"),
        P("tensor", None),
        P(),
    )
    return jax.shard_map(shards, mesh=mesh, in_specs=in_specs, out_specs=out_specs, check_vma=False)
```

```python
from functools import partial

import jax
import jax.numpy as jnp
from jax import lax
from jax.experimental import pallas as pl
from jax.experimental.pallas import tpu as pltpu
from jax.sharding import PartitionSpec as P

norm_eps = 1e-06
MESH = pl.DeviceIdType.MESH
f32, bf16 = jnp.float32, jnp.bfloat16


def dot(left, right):
    return jnp.dot(left, right, preferred_element_type=f32)


def dot_nt(left, right):
    return lax.dot_general(left, right, (((1,), (1,)), ((), ())), preferred_element_type=f32)


def dot_tn(left, right):
    return lax.dot_general(left, right, (((0,), (0,)), ((), ())), preferred_element_type=f32)


def two_part(left, right):
    high = right.astype(bf16)
    rest = (right - high.astype(f32)).astype(bf16)
    return dot(left, high) + dot(left, rest)


def ones_where(same):
    return jnp.where(same, 1.0, 0.0).astype(bf16)


def iota(shape, dim):
    return lax.broadcasted_iota(jnp.int32, shape, dim)


def hat(values):
    center = values - jnp.mean(values, axis=-1, keepdims=True)
    scale = lax.rsqrt(jnp.mean(center * center, axis=-1, keepdims=True) + norm_eps)
    return center * scale, scale


def sigmoid(v):
    return 1.0 / (1.0 + jnp.exp(-v))


def norm_back(hatted, scale, grad):
    inner = jnp.mean(grad * hatted, axis=-1, keepdims=True)
    return scale * (grad - jnp.mean(grad, axis=-1, keepdims=True) - hatted * inner)


def column_sum(values):
    return jnp.sum(values, axis=0, keepdims=True)


class Grid:
    def __init__(self, images, side, width):
        self.images, self.side, self.width = images, side, width
        self.stride = -(-side // 8) * 8
        self.lines = 8 if side % 8 == 0 else side
        self.chunk = self.lines * self.stride
        self.per_image = side // self.lines
        self.rows = images * side * self.stride
        self.chunks = self.rows // self.chunk
        self.tall = (side + 1) * self.stride
        self.padded = images * self.tall + self.stride
        self.full = self.stride == side

    def here(self, index):
        return pl.ds(pl.multiple_of(index * self.chunk, 8), self.chunk)

    def at(self, index):
        return index // self.per_image * self.tall + index % self.per_image * self.chunk + self.stride

    def bordered(self, index, line=0):
        return pl.ds(pl.multiple_of(self.at(index) + line * self.stride, 8), self.chunk)

    def cells_only(self, values):
        if self.full:
            return values
        return jnp.where(iota(values.shape, 0) % self.stride < self.side, values, 0.0)


def clear_borders(grid, spread):
    for image in range(grid.images + 1):
        border = pl.ds(image * grid.tall, grid.stride)
        spread[border, 0 : 3 * grid.width] = jnp.zeros((grid.stride, 3 * grid.width), f32)


def spread_columns(grid, spread):
    width, size = grid.width, grid.chunk

    def one(i, _):
        start = pl.multiple_of(grid.at(i) - 8, 8)
        middle = spread[pl.ds(start, size + 16), width : 2 * width]
        left = pltpu.roll(middle, 1, 0)[8 : 8 + size]
        right = pltpu.roll(middle, size + 15, 0)[8 : 8 + size]
        if grid.full:
            column = iota((size, width), 0) % grid.stride
            left = jnp.where(column == 0, 0.0, left)
            right = jnp.where(column == grid.side - 1, 0.0, right)
        spread[grid.bordered(i), 0:width] = left
        spread[grid.bordered(i), 2 * width : 3 * width] = right
        return 0

    lax.fori_loop(0, grid.chunks, one, 0)


def block_forward(grid, load, params, reduced, convolved, spread, emit):
    weight, gain1, bias1, kernel, gain2, bias2, expand, gain3, bias3 = params
    width = grid.width
    clear_borders(grid, spread)

    def first(i, _):
        value = dot(load(i).astype(bf16), weight[...])
        reduced[grid.here(i), :] = value
        normed = hat(value)[0] * gain1[...] + bias1[...]
        low = (normed * sigmoid(normed)).astype(bf16).astype(f32)
        spread[grid.bordered(i), width : 2 * width] = grid.cells_only(low)
        return 0

    lax.fori_loop(0, grid.chunks, first, 0, unroll=2)
    spread_columns(grid, spread)

    def second(i, _):
        total = dot(spread[grid.bordered(i, -1), 0 : 3 * width].astype(bf16), kernel[0])
        total += dot(spread[grid.bordered(i, 0), 0 : 3 * width].astype(bf16), kernel[1])
        total += dot(spread[grid.bordered(i, 1), 0 : 3 * width].astype(bf16), kernel[2])
        convolved[grid.here(i), :] = total
        normed = hat(total)[0] * gain2[...] + bias2[...]
        expanded = dot((normed * sigmoid(normed)).astype(bf16), expand[...])
        emit(i, load(i).astype(f32) + hat(expanded)[0] * gain3[...] + bias3[...])
        return 0

    lax.fori_loop(0, grid.chunks, second, 0, unroll=2)


def block_backward(grid, load, load_grad, params, reduced, convolved, spread, grads, emit, cuts):
    weight, gain1, bias1, kernel, gain2, bias2, expand, gain3, bias3 = params
    d_weight, d_gain1, d_bias1, d_kernel, d_gain2, d_bias2, d_expand, d_gain3, d_bias3 = grads
    width = grid.width
    for ref in grads:
        ref[...] = jnp.zeros(ref.shape, f32)
    clear_borders(grid, spread)

    def first(i, _):
        hat2, scale2 = hat(convolved[grid.here(i), :])
        normed = hat2 * gain2[...] + bias2[...]
        sig = sigmoid(normed)
        middle = (normed * sig).astype(bf16)
        hat3, scale3 = hat(dot(middle, expand[...]))
        grad = load_grad(i)
        d_gain3[...] += column_sum(grad * hat3)
        d_bias3[...] += column_sum(grad)
        grad_expanded = norm_back(hat3, scale3, grad * gain3[...]).astype(bf16)
        d_expand[...] += dot_tn(middle, grad_expanded)
        grad_normed = dot_nt(grad_expanded, expand[...]) * (sig * (1.0 + normed * (1.0 - sig)))
        d_gain2[...] += column_sum(grad_normed * hat2)
        d_bias2[...] += column_sum(grad_normed)
        grad_convolved = norm_back(hat2, scale2, grad_normed * gain2[...])
        spread[grid.bordered(i), width : 2 * width] = grad_convolved.astype(bf16).astype(f32)
        return 0

    for low, high in cuts[0]:
        lax.fori_loop(low, high, first, 0)
        if high == grid.chunks:
            spread_columns(grid, spread)
        yield

    def second(i, _):
        hat1, scale1 = hat(reduced[grid.here(i), :])
        normed = hat1 * gain1[...] + bias1[...]
        sig = sigmoid(normed)
        active = grid.cells_only(normed * sig).astype(bf16)
        total = None
        for line in range(3):
            moved = spread[grid.bordered(i, line - 1), 0 : 3 * width].astype(bf16)
            part = dot_tn(active, moved)
            for col in range(3):
                cols = slice(col * width, (col + 1) * width)
                tap = (2 - line) * 3 + 2 - col
                d_kernel[tap * width : (tap + 1) * width, :] += part[:, cols]
                back = kernel[2 - line, (2 - col) * width : (3 - col) * width, :]
                product = dot_nt(moved[:, cols], back)
                total = product if total is None else total + product
        grad_normed = grid.cells_only(total * (sig * (1.0 + normed * (1.0 - sig))))
        d_gain1[...] += column_sum(grad_normed * hat1)
        d_bias1[...] += column_sum(grad_normed)
        grad_reduced = norm_back(hat1, scale1, grad_normed * gain1[...]).astype(bf16)
        d_weight[...] += dot_tn(load(i).astype(bf16), grad_reduced)
        emit(i, load_grad(i) + dot_nt(grad_reduced, weight[...]))
        return 0

    for low, high in cuts[1]:
        lax.fori_loop(low, high, second, 0)
        yield


def pool_matrix(early, late, down):
    cells = early.lines // 2 * late.stride
    shape = (cells, early.chunk) if down else (early.chunk, cells)
    big, small = iota(shape, 1 if down else 0), iota(shape, 0 if down else 1)
    same_line = big // (2 * early.stride) == small // late.stride
    return ones_where(same_line & (big % early.stride // 2 == small % late.stride))


def token_matrix(late, starts, first, rows, down):
    shape = (rows, late.rows) if down else (late.chunk, rows)
    packed, cell = iota(shape, 0 if down else 1), iota(shape, 1 if down else 0)
    if down:
        packed += first
    else:
        cell += first
    inside = cell % (late.side * late.stride)
    line, column = inside // late.stride, inside % late.stride
    image = cell // (late.side * late.stride)
    start = jnp.zeros(shape, jnp.int32)
    for n in range(late.images):
        start = jnp.where(image == n, starts[n], start)
    return ones_where((packed == start + line * late.side + column) & (column < late.side))


PIECES = 16
RING = 8
RING_LINES = 4


class Plan:
    def __init__(self, images, side, channels, width, group, ring, hidden, out):
        self.early, self.late = Grid(images, side, width), Grid(images, side // 2, width)
        self.images, self.channels, self.width, self.out = images, channels, width, out
        self.span = (side // 2) ** 2
        self.block = images * self.span
        self.group, self.chips = group, group // 2
        self.rows = group * self.block
        self.ring = ring == RING and group == 4
        self.hidden = hidden
        self.piece = out // PIECES
        self.slab = channels // PIECES
        taps = 9 * width
        self.kernel_at = (0, taps)
        self.reduce_at = (2 * taps, 2 * taps + channels)
        self.expand_at = (2 * taps + 2 * channels, 2 * taps + 3 * channels)
        self.small_at = 2 * taps + 4 * channels
        self.small_block = 4 + 2 * channels // width
        self.small = 2 * self.small_block + out // width + group * hidden // width
        self.flat_piece = -(-(self.small_at + self.small) // (group * PIECES * 16)) * 16
        self.flat = group * PIECES * self.flat_piece


def ring_place(device):
    line, column = device // 2, lax.rem(device, 2)
    return (1 - column) * line + column * (2 * RING_LINES - 1 - line)


def ring_device(place):
    column = place // RING_LINES
    return 2 * ((1 - column) * place + column * (2 * RING_LINES - 1 - place)) + column


class Ring:
    def __init__(self, place, held, first, out, sems, local, window, tap=None):
        self.place, self.held, self.first, self.out = place, held, first, out
        self.sems, self.local, self.window, self.tap = sems, local, window, tap
        ahead = ring_device(lax.rem(place + 1, RING))
        behind = ring_device(lax.rem(place + RING - 1, RING))
        self.to = (ahead, behind)

    def index(self, way, step):
        turn = self.place - step if way == 0 else self.place + step
        return way * RING + lax.rem(turn + 2 * RING, RING)

    def landed(self, index):
        return self.out.at[index, self.window, :]

    def copy(self, way, step, gather):
        if gather:
            target = self.landed(self.index(way, step - 1))
            source = self.held.at[way, RING - 2, self.window, :] if step == 0 else target
        else:
            source = self.first.at[way, self.window, :]
            if step:
                source = self.held.at[way, step - 1, self.window, :]
            target = self.held.at[way, step, self.window, :]
        return pltpu.make_async_remote_copy(
            src_ref=source,
            dst_ref=target,
            send_sem=self.sems[2 * gather].at[way, step],
            recv_sem=self.sems[2 * gather + 1].at[way, step],
            device_id={"dp": self.to[way]},
            device_id_type=MESH,
        )

    def keep(self, way):
        source = self.held.at[way, RING - 2, self.window, :]
        return pltpu.make_async_copy(source, self.landed(self.index(way, -1)), self.local.at[way])

    def reduce(self, step, partial):
        for way in range(2):
            if step:
                self.copy(way, step - 1, 0).wait_recv()
            target = self.first.at[way] if step == 0 else self.held.at[way, step - 1]

            def put(window, value, target=target):
                if step:
                    value = value + target[window].astype(f32)
                target[window] = value.astype(bf16)

            partial(way, self.index(way, step), put)
            if step < RING - 1:
                self.copy(way, step, 0).start()
            else:
                self.copy(way, 0, 1).start()
                self.keep(way).start()
                if self.tap:
                    self.tap(way, 0, self.index(way, -1), self.held.at[way, RING - 2, self.window, :])

    def gather(self, step):
        for way in range(2):
            self.copy(way, step - 1, 1).wait_recv()
            index = self.index(way, step - 1)
            if step < RING - 1:
                self.copy(way, step, 1).start()
            if self.tap:
                self.tap(way, step, index, self.landed(index))

    def tick(self, count, partial):
        if count < RING:
            self.reduce(count, partial)
        else:
            self.gather(count - RING + 1)

    def finish(self):
        for way in range(2):
            self.keep(way).wait()
            for step in range(RING - 1):
                self.copy(way, step, 0).wait_send()
                self.copy(way, step, 1).wait_send()


TICKS = 2 * RING - 1
SUBS = 2
UNPACK_STEPS = 16
AHEAD = 2
STREAMED = ("xs", "early0", "early3", "early6", "late0", "late3", "late6", "win")


def mega(plan, names, *all_refs):
    r = dict(zip(names, all_refs))
    early, late, block, chips, group = plan.early, plan.late, plan.block, plan.chips, plan.group
    hid, out, piece, ch, width = plan.hidden, plan.out, plan.piece, plan.channels, plan.width
    me = lax.axis_index("tensor")
    chip, core = me // 2, lax.rem(me, 2)
    place = ring_place(lax.axis_index("dp")) if plan.ring else 0 * me
    pair = {"tensor": 2 * chip + 1 - core}
    ep, lp = ([r[f"{name}{k}"] for k in range(9)] for name in ("early", "late"))

    def other(hop):
        return {"tensor": 2 * lax.rem(chip + hop + chips, chips) + core}

    started = []

    def send(source, target, name, at, device):
        return pltpu.make_async_remote_copy(
            src_ref=source,
            dst_ref=target,
            send_sem=r[name + "_s"].at[at],
            recv_sem=r[name + "_r"].at[at],
            device_id=device,
            device_id_type=MESH,
        )

    def go(copy, keep=True):
        copy.start()
        if keep:
            started.append(copy)

    def order(step):
        back, forth = lax.rem(place - step + 2 * RING, RING), lax.rem(place + step, RING)
        return (back, RING + forth)

    def columns(index, size):
        return pl.ds(pl.multiple_of(index * size, 128), size)

    def rows_at(index, size):
        return pl.ds(pl.multiple_of(index * size, 16), size)

    sems = [r[f"ring_{kind}"] for kind in ("rs", "rr", "gs", "gr")]

    def ring_of(n, held, first, target, window, tap=None):
        mine = [sem.at[n] for sem in sems]
        return Ring(place, held, first, target, mine, r["ring_l"].at[n], window, tap)

    gflat = r["gflat"]

    def to_pair(hop, way, step, index, source):
        target = gflat.at[core, lax.rem(chip - hop + chips, chips), index]
        return send(source, target, "ac", (hop, way, step), pair)

    def spread_piece(way, step, index, source):
        for hop in range(1, chips):
            go(send(source, gflat.at[core, chip, index], "ax", (hop - 1, way, step), other(hop)))
        go(to_pair(0, way, step, index, source))

    part_rows = hid // SUBS
    one = [
        ring_of(k, r["held"], r["first"], r["gout"], pl.ds(k * part_rows, part_rows)) for k in range(SUBS)
    ]
    two = ring_of(SUBS, r["held2"], r["first2"], r["gin"], pl.ds(0, plan.slab))
    three = None
    if plan.ring:
        whole = pl.ds(0, plan.flat_piece)
        three = ring_of(SUBS + 1, r["held3"], r["first3"], gflat.at[core, chip], whole, spread_piece)

    loads = {}
    for k, name in enumerate(STREAMED):
        loads[name] = pltpu.make_async_copy(r[name + "_in"], r[name], r["pload"].at[k])

    def loaded(*names):
        for name in names:
            loads[name].wait()

    for name in ("xs", "early0", "early3", "early6"):
        loads[name].start()
    barrier = pltpu.get_barrier_semaphore()
    friends = [pair] + [other(hop) for hop in range(1, chips)]
    if plan.ring:
        friends += [{"dp": two.to[0]}, {"dp": two.to[1]}]
    for friend in friends:
        pl.semaphore_signal(barrier, inc=1, device_id=friend, device_id_type=MESH)
    pl.semaphore_wait(barrier, len(friends))

    cot, gall = r["cot"], r["gall"]

    def cot_own(step):
        for way, index in enumerate(order(step)):
            go(send(cot.at[:, columns(index, piece)], gall.at[1, index], "cc", (0, step, way), pair))

    def cot_far(step):
        for hop in range(1, chips):
            for way, index in enumerate(order(step)):
                source = cot.at[:, columns(index, piece)]
                go(send(source, gall.at[2 * hop, index], "cx", (hop - 1, step, way), other(hop)))

    def cot_pass(step):
        for hop in range(1, chips):
            for way, index in enumerate(order(step)):
                source = gall.at[2 * hop, index]
                send(source, source, "cx", (hop - 1, step, way), other(hop)).wait_recv()
                go(send(source, gall.at[2 * hop + 1, index], "cc", (hop, step, way), pair))

    ready = set()

    def cot_ready(step):
        if step in ready:
            return
        ready.add(step)
        for hop in range(chips):
            for way, index in enumerate(order(step)):
                target = gall.at[2 * hop + 1, index]
                send(target, target, "cc", (hop, step, way), pair).wait_recv()

    for step in range(AHEAD):
        cot_far(step)
    for name in ("late0", "late3", "late6", "win"):
        loads[name].start()
    for step in range(RING):
        cot_own(step)
    for name in ("bin", "bout"):
        source = r[name][...].astype(f32)
        for k in range(source.shape[0]):
            r[name + "_wide"][:, k * 128 : (k + 1) * 128] = source[k : k + 1, :]
    loaded("xs", "early0", "early3", "early6")

    xs, pool, act, tok, big = r["xs"], r["pool"], r["act"], r["tok"], r["big"]
    cells = early.lines // 2 * late.stride

    def load_early(i):
        return xs[early.here(i), :]

    def load_late(i):
        return pool[late.here(i), :]

    def put_early(i, value):
        pool[rows_at(i, cells), :] = two_part(pool_matrix(early, late, True), value) * 0.25

    tsend, tpair, tfar = r["tsend"], r["tpair"], r["tfar"]

    def put_late(i, value):
        tsend[i, 0 : late.chunk, :] = value.astype(bf16)

    block_forward(early, load_early, ep, r["ered"], r["econv"], big, put_early)
    loaded("late0", "late3", "late6", "win")
    block_forward(late, load_late, lp, r["lred"], r["lconv"], big, put_late)
    span = plan.span
    token_sends = []

    def token_copy(source, target, name, hop, n, device):
        rows = pl.ds(n * span, span)
        return send(tok.at[source, rows, :], tok.at[target, rows, :], name, (hop, n), device)

    def token_far(hop, n):
        return token_copy(0, 2 * hop, "tx", hop - 1, n, other(hop))

    def token_pair(hop, n):
        return token_copy(2 * hop, 2 * hop + 1, "tc", hop, n, pair)

    for n in range(plan.images):
        matrix = token_matrix(late, r["starts"], n * span, span, True)
        value = None
        for i in range(late.chunks):
            part = dot(matrix[:, i * late.chunk : (i + 1) * late.chunk], tsend[i, 0 : late.chunk, :])
            value = part if value is None else value + part
        tok[0, n * span : (n + 1) * span, :] = value.astype(bf16)
        token_sends += [token_far(hop, n) for hop in range(1, chips)] + [token_pair(0, n)]
        for copy in token_sends[-chips:]:
            copy.start()
    for step in range(AHEAD, RING):
        cot_far(step)
    for step in range(AHEAD - 1):
        cot_pass(step)

    slope, win = r["slope"], r["win"]

    def hidden_of(j, n):
        rows = pl.ds(j * block + n * span, span)

        def body(q, _):
            cols = columns(q, 256)
            pre = dot(tok[j, n * span : (n + 1) * span, :], win[:, cols]) + r["bin_wide"][:, cols]
            bend = jnp.tanh(0.7978845608 * (pre + 0.044715 * pre * pre * pre))
            act[rows, cols] = (0.5 * pre * (1.0 + bend)).astype(bf16)
            rise = 0.7978845608 * (1.0 + 3.0 * 0.044715 * pre * pre)
            slope[rows, cols] = (0.5 * (1.0 + bend) + 0.5 * pre * (1.0 - bend * bend) * rise).astype(bf16)
            return 0

        lax.fori_loop(0, hid // 256, body, 0)

    for n in range(plan.images):
        hidden_of(0, n)
    for n in range(plan.images):
        token_pair(0, n).wait_recv()
        hidden_of(1, n)
    cot_pass(AHEAD - 1)
    for hop in range(1, chips):
        for n in range(plan.images):
            token_far(hop, n).wait_recv()
            token_sends.append(token_pair(hop, n))
            token_sends[-1].start()
            hidden_of(2 * hop, n)
            token_pair(hop, n).wait_recv()
            hidden_of(2 * hop + 1, n)

    turned, gbuf = r["turned"], r["gbuf"]

    def turn(i, _):
        stripe = act[:, columns(i, 128)].astype(f32)
        turned[rows_at(i, 128), :] = jnp.transpose(stripe).astype(bf16)
        return 0

    lax.fori_loop(0, hid // 128, turn, 0)

    def cot_piece(j, index):
        return cot.at[:, columns(index, piece)] if j == 0 else gall.at[j, index]

    def piece_loads(step, way):
        slot, index = step % 2, order(step)[way]
        loads = []
        for j in range(group):
            target = gbuf.at[slot, way, pl.ds(j * block, block), :]
            loads.append(pltpu.make_async_copy(cot_piece(j, index), target, r["gload"].at[slot, way, j]))
        return loads

    def prepare(step):
        cot_ready(step)
        for way in range(2):
            for load in piece_loads(step, way):
                load.start()

    def piece_of(step, sub):
        def partial(way, index, put):
            tile = gbuf.at[step % 2, way]
            if sub == 0:
                for load in piece_loads(step, way):
                    load.wait()

            def body(i, _):
                rows = pl.ds(pl.multiple_of(sub * part_rows + i * 256, 256), 256)
                put((rows, slice(None)), dot(turned[rows, :], tile[...]))
                return 0

            lax.fori_loop(0, part_rows // 256, body, 0)

        return partial

    def alone(step, ring, partial):
        for way, index in enumerate(order(step)):
            stage = ring.first.at[way]

            def put(window, value, stage=stage):
                stage[window] = value.astype(bf16)

            partial(way, index, put)
            write = pltpu.make_async_copy(stage.at[ring.window, :], ring.landed(index), ring.local.at[way])
            write.start()
            write.wait()

    def tick(ring, count, partial):
        if plan.ring:
            ring.tick(count, partial)
        elif count < RING:
            alone(count, ring, partial)

    def tick_one(count):
        step, sub = count // SUBS, count % SUBS
        tick(one[sub], step, piece_of(step, sub))
        if sub == 0 and step + 1 < RING:
            prepare(step + 1)

    wout, wbuf, rbuf = r["wout"], r["wbuf"], r["rbuf"]
    tiles = out // piece

    def result_pass(blocks, extra, finish, low, high):
        def loads(i, slot):
            cols = columns(i, piece)
            pairs = [(wout.at[:, cols], wbuf.at[slot])]
            for n, ref in enumerate(extra):
                pairs.append((ref.at[:, cols], turned.at[pl.ds(n * block, block), columns(slot, piece)]))
            return [pltpu.make_async_copy(a, b, r["wload"].at[slot, n]) for n, (a, b) in enumerate(pairs)]

        for k in range(3):
            for load in loads(low + k, k):
                load.start()

        def body(k, _):
            i, slot = low + k, lax.rem(k, 4)
            for load in loads(i, slot):
                load.wait()

            @pl.when(i + 3 < high)
            def _():
                for load in loads(i + 3, lax.rem(k + 3, 4)):
                    load.start()

            for n, j in enumerate(blocks):
                value = dot(act[j * block : (j + 1) * block, :], wbuf[slot])
                for m in range(len(extra)):
                    value += turned[m * block : (m + 1) * block, columns(slot, piece)].astype(f32)
                finish(n, i, value)
            return 0

        lax.fori_loop(0, high - low, body, 0)

    def pair_copy(hop):
        return send(rbuf.at[hop], r["rpair"].at[hop], "rp", (hop,), pair)

    def result_pairs(low, high):
        def put(n, i, value):
            rbuf[n, :, columns(i, piece)] = value.astype(bf16)

        result_pass([2 * hop + 1 for hop in range(chips)], [], put, low, high)
        if high == tiles:
            for hop in range(chips):
                go(pair_copy(hop), False)

    def result_pairs_done():
        for hop in range(chips):
            pair_copy(hop).wait()

    def result_far():
        for hop in range(chips - 1, 0, -1):
            extra = [r["rpair"].at[hop]]
            if hop < chips - 1:
                send(rbuf.at[0], r["rfar"].at[hop], "rx", (hop,), other(-1)).wait_recv()
                extra.append(r["rfar"].at[hop])

            def put(n, i, value, hop=hop):
                rbuf[hop, :, columns(i, piece)] = value.astype(bf16)

            result_pass([2 * hop], extra, put, 0, tiles)
            go(send(rbuf.at[hop], r["rfar"].at[hop - 1], "rx", (hop - 1,), other(-1)))

    def result_own():
        send(rbuf.at[0], r["rfar"].at[0], "rx", (0,), other(-1)).wait_recv()

        def put(n, i, value):
            cols = columns(i, piece)
            rbuf[0, :, cols] = (value + r["bout_wide"][:, cols]).astype(bf16)

        result_pass([0], [r["rpair"].at[0], r["rfar"].at[0]], put, 0, tiles)
        go(pltpu.make_async_copy(rbuf.at[0], r["projected"], r["load"].at[1]))

    flat = r["flat"]
    rows_all = plan.rows

    def active_rows(slot, way, j):
        return rows_at(2 * slot + way, rows_all) if j is None else pl.ds(
            pl.multiple_of((2 * slot + way) * rows_all + j * block, 16), block
        )

    def active_loads(step, slot):
        loads = []
        for way, index in enumerate(order(step)):
            for j in range(group):
                target = flat.at[active_rows(slot, way, j), :]
                sem = r["aload"].at[slot, way, j]
                loads.append(pltpu.make_async_copy(cot_piece(j, index), target, sem))
            sem = r["aload"].at[slot, way, group]
            target = wbuf.at[2 * slot + way]
            loads.append(pltpu.make_async_copy(wout.at[:, columns(index, piece)], target, sem))
        return loads

    def active_steps(low, high):
        if low == 0:
            for load in active_loads(0, 0):
                load.start()

        def body(step, _):
            slot = lax.rem(step, 2)
            for load in active_loads(step, slot):
                load.wait()

            @pl.when(step + 1 < RING)
            def _():
                for load in active_loads(step + 1, 1 - slot):
                    load.start()

            for way, index in enumerate(order(step)):
                own = flat[active_rows(slot, way, 0), :].astype(f32)
                r["outbias"][pl.ds(index, 1), :] = column_sum(own)

            def rows_of(j, _):
                rows = rows_at(j, block)
                value = dot_nt(flat[active_rows(slot, 0, j), :], wbuf[2 * slot])
                value += dot_nt(flat[active_rows(slot, 1, j), :], wbuf[2 * slot + 1])
                before = big[rows, 0:hid]
                big[rows, 0:hid] = value + (jnp.where(step == 0, 0.0, before) if low == 0 else before)
                return 0

            lax.fori_loop(0, group, rows_of, 0)
            return 0

        lax.fori_loop(low, high, body, 0)

    def hidden_back():
        r["inbias"][...] = jnp.zeros(r["inbias"].shape, f32)

        def body(i, _):
            rows = rows_at(i, block // 2)
            value = (big[rows, 0:hid] * slope[rows, :].astype(f32)).astype(bf16)
            slope[rows, :] = value
            r["inbias"][...] += column_sum(value.astype(f32))
            return 0

        lax.fori_loop(0, 2 * group, body, 0)

    def tokens_pair(hop):
        return send(tsend.at[hop], tpair.at[hop], "gc", (hop,), pair)

    def tokens_far_copy(hop):
        return send(tsend.at[hop], tfar.at[hop - 1], "gx_", (hop - 1,), other(-1))

    def tokens_tile(j, q):
        return dot_nt(slope[j * block : (j + 1) * block, :], win[rows_at(q, 256), :])

    def tokens_fetch(*sources):
        loads = []
        for n, source in enumerate(sources):
            for q in range(ch // 256):
                target = flat.at[pl.ds((n * (ch // 256) + q) * block, block), :]
                sem = r["tload"].at[n, q]
                loads.append(pltpu.make_async_copy(source.at[:, pl.ds(q * 256, 256)], target, sem))
        for load in loads:
            load.start()
        for load in loads:
            load.wait()

    def tokens_sum(j, q, count):
        value = tokens_tile(j, q)
        for n in range(count):
            value += flat[rows_at(n * (ch // 256) + q, block), :].astype(f32)
        return value

    def tokens_out(hop, j, count):
        def body(q, _):
            tsend[hop, :, columns(q, 256)] = tokens_sum(j, q, count).astype(bf16)
            return 0

        lax.fori_loop(0, ch // 256, body, 0)

    def tokens_far():
        for hop in range(chips - 1, -1, -1):
            tokens_out(hop, 2 * hop + 1, 0)
            go(tokens_pair(hop), False)
        for hop in range(chips - 1, 0, -1):
            tokens_pair(hop).wait()
            sources = [tpair.at[hop]]
            if hop < chips - 1:
                tokens_far_copy(hop + 1).wait_recv()
                sources.append(tfar.at[hop])
            tokens_fetch(*sources)
            tokens_out(hop, 2 * hop, len(sources))
            go(tokens_far_copy(hop))

    def tokens_own():
        tokens_pair(0).wait()
        tokens_far_copy(1).wait_recv()
        tokens_fetch(tpair.at[0], tfar.at[0])

        def body(q, _):
            value = tokens_sum(0, q, 2)
            for i in range(late.chunks):
                matrix = token_matrix(late, r["starts"], i * late.chunk, block, False)
                r["gpool"][i * late.chunk : (i + 1) * late.chunk, columns(q, 256)] = two_part(matrix, value)
            return 0

        lax.fori_loop(0, ch // 256, body, 0)

    parts = hid // 256

    def weights_in():
        for copy in token_sends:
            copy.wait_send()

        def body(i, _):
            total = None
            for j in range(group):
                part = dot_tn(tok[j, :, columns(i, 256)], slope[j * block : (j + 1) * block, :])
                total = part if total is None else total + part
            for q in range(parts):
                tok[q, 0:256, columns(i, 256)] = total[:, q * 256 : (q + 1) * 256].astype(bf16)
            return 0

        lax.fori_loop(0, ch // 256, body, 0)

    def slab_of(way, index, put):
        each = 256 // plan.slab
        for q in range(parts):
            value = tok[q, rows_at(lax.rem(index, each), plan.slab), columns(index // each, 256)]
            put((slice(None), slice(q * 256, (q + 1) * 256)), value.astype(f32))

    def tick_two(count):
        tick(two, count, slab_of)

    gpool = r["gpool"]
    acc = [r[f"acc{k}"] for k in range(9)]

    def late_back():
        def put(i, value):
            gpool[late.here(i), :] = value * 0.25

        def grad(i):
            return gpool[late.here(i), :]

        cuts = [[(0, late.chunks)]] * 2
        return block_backward(late, load_late, grad, lp, r["lred"], r["lconv"], big, acc, put, cuts)

    def early_back():
        def grad(i):
            return two_part(pool_matrix(early, late, False), gpool[rows_at(i, cells), :])

        def put(i, value):
            xs[early.here(i), :] = value.astype(bf16)

        count = early.chunks
        cuts = [[(0, count // 2), (count // 2, count)]]
        cuts.append([(k * count // 3, (k + 1) * count // 3) for k in range(3)])
        return block_backward(early, load_early, grad, ep, r["ered"], r["econv"], big, acc, put, cuts)

    small = r["small"]

    def store_flat(n):
        flat[pl.ds(plan.kernel_at[n], 9 * width), :] = acc[3][...].astype(bf16)
        flat[pl.ds(plan.reduce_at[n], ch), :] = acc[0][...].astype(bf16)
        quarters = ch // width
        for q in range(quarters):
            rows = pl.ds(plan.expand_at[n] + q * width, width)
            flat[rows, :] = acc[6][:, q * width : (q + 1) * width].astype(bf16)
        at = n * plan.small_block
        for k, ref in enumerate((acc[1], acc[2], acc[4], acc[5])):
            small[at + k : at + k + 1, :] = ref[...]
        for k, ref in enumerate((acc[7], acc[8])):
            for q in range(quarters):
                row = at + 4 + k * quarters + q
                small[row : row + 1, :] = ref[:, q * width : (q + 1) * width]

    def store_small():
        at = 2 * plan.small_block
        small[at : at + out // width, :] = r["outbias"][...]
        at += out // width
        for owner in range(group):
            for q in range(hid // width):
                row = at + owner * (hid // width) + q
                part = r["inbias"][:, q * width : (q + 1) * width]
                small[row : row + 1, :] = jnp.where(me == owner, part, 0.0)
        row = at + group * hid // width
        small[row:, :] = jnp.zeros((small.shape[0] - row, width), f32)
        flat[pl.ds(plan.small_at, small.shape[0]), :] = small[...].astype(bf16)
        rest = plan.small_at + small.shape[0]
        flat[pl.ds(rest, plan.flat - rest), :] = jnp.zeros((plan.flat - rest, width), bf16)

    half, quarter = plan.flat // 2, plan.flat // group
    flat_piece = plan.flat_piece

    def flat_pair():
        away = flat.at[rows_at(1 - core, half), :]
        return send(away, r["fpair"], "fp", (0,), pair)

    def flat_far_copy(hop):
        return send(gbuf.at[1], r["ffar"], "fx", (hop - 1,), other(hop))

    def own_piece(index):
        across = big.shape[1] // width
        return rows_at(index // across, flat_piece), columns(lax.rem(index, across), width)

    upper = PIECES // 2

    def stage(sources):
        loads = [
            pltpu.make_async_copy(source, gbuf.at[0, n], r["load"].at[2 + n])
            for n, source in enumerate(sources)
        ]
        for load in loads:
            load.start()
        for load in loads:
            load.wait()

    def staged(i):
        return (i // upper, rows_at(lax.rem(i, upper), flat_piece))

    def flat_far():
        flat_pair().wait_recv()
        for hop in range(chips - 1, -1, -1):
            to = lax.rem(chip + hop, chips)
            stage([r["fpair"].at[rows_at(2 * to + n, quarter // 2), :] for n in range(2)])

            def body(i, _, hop=hop, to=to):
                mine = pl.ds(pl.multiple_of(core * half + to * quarter + i * flat_piece, 16), flat_piece)
                total = flat[mine, :].astype(f32) + gbuf[(0, *staged(i))].astype(f32)
                if hop:
                    gbuf[(1, *staged(i))] = total.astype(bf16)
                else:
                    big[own_piece(i)] = total
                return 0

            lax.fori_loop(0, PIECES, body, 0)
            if hop:
                go(flat_far_copy(hop))

    def flat_sum():
        for hop in range(1, chips):
            flat_far_copy(hop).wait_recv()
            stage([r["ffar"].at[n] for n in range(2)])

            def body(i, _):
                big[own_piece(i)] += gbuf[(0, *staged(i))].astype(f32)
                return 0

            lax.fori_loop(0, PIECES, body, 0)

    def flat_of(way, index, put):
        put((slice(None), slice(None)), big[own_piece(index)])

    def tick_three(count):
        tick(three, count, flat_of)

    def flat_spread():
        for hop in range(1, chips):
            theirs = gflat.at[core, lax.rem(chip - hop + chips, chips)]
            for step in range(RING):
                for way in range(2):
                    index = three.index(way, step - 1)
                    ref = theirs.at[index]
                    send(ref, ref, "ax", (hop - 1, way, step), other(hop)).wait_recv()
                    go(to_pair(hop, way, step, index, ref))
        for hop in range(chips):
            for step in range(RING):
                for way in range(2):
                    index = three.index(way, step - 1)
                    to_pair(hop, way, step, index, gflat.at[core, 0, index]).wait_recv()

    def early_ready(low, high):
        for step in range(low, high):
            cot_ready(step)

    prepare(0)
    tick_one(0)
    tick_one(1)
    cot_pass(2)
    early_ready(0, 2)
    active_steps(0, 1)
    early_ready(0, 3)
    active_steps(1, 2)
    cot_pass(3)
    tick_one(2)
    early_ready(0, 4)
    active_steps(2, 3)
    cot_pass(4)
    tick_one(3)
    early_ready(0, 5)
    active_steps(3, 4)
    cot_pass(5)
    tick_one(4)
    early_ready(0, 6)
    active_steps(4, 5)
    cot_pass(6)
    tick_one(5)
    early_ready(0, 7)
    active_steps(5, 6)
    cot_pass(7)
    tick_one(6)
    early_ready(0, RING)
    active_steps(6, RING)
    hidden_back()
    tokens_far()
    tick_one(7)
    weights_in()
    tick_one(8)
    result_pairs(0, tiles // 2)
    tick_one(9)
    tokens_own()
    tick_two(0)
    part = late_back()
    next(part)
    tick_one(10)
    next(part)
    store_flat(1)
    tick_one(11)
    part = early_back()
    next(part)
    tick_two(1)
    tick_one(12)
    next(part)
    tick_one(13)
    next(part)
    tick_two(2)
    tick_one(14)
    next(part)
    tick_one(15)
    next(part)
    go(pltpu.make_async_copy(xs, r["gx"], r["load"].at[0]))
    store_flat(0)
    store_small()
    if plan.ring:
        go(flat_pair())
    else:
        go(pltpu.make_async_copy(flat, gflat, r["load"].at[2]))
    tick_two(3)
    tick_one(16)
    if plan.ring:
        flat_far()
    tick_one(17)
    result_pairs(tiles // 2, tiles)
    tick_two(4)
    tick_one(18)
    result_pairs_done()
    result_far()
    tick_two(5)
    later = 0
    for count in range(19, SUBS * TICKS):
        tick_one(count)
        if count - 13 < TICKS:
            tick_two(count - 13)
        if plan.ring and count == 19:
            flat_sum()
        for _ in range(2 if plan.ring else 0):
            if later < TICKS:
                tick_three(later)
                later += 1
        if count == SUBS * TICKS - 4:
            result_own()
        if count == SUBS * TICKS - 3 and plan.ring:
            three.finish()
            flat_spread()
    if plan.ring:
        for ring in (*one, two):
            ring.finish()
    for copy in started:
        if copy.is_remote:
            copy.wait_send()
        else:
            copy.wait()


def unpack_body(group, gout, gin, gx, kernel0, kernel1, reduce0, reduce1, expand0, expand1, small, *outs):
    big_outs, small_outs = outs[:9], outs[9:]
    size = gout.shape[2]
    for piece in range(PIECES):
        big_outs[0][:, piece * size : (piece + 1) * size] = gout[piece].astype(f32)
    big_outs[1][...] = gin[...].astype(f32)
    for source, target in zip((gx, kernel0, kernel1, reduce0, reduce1, expand0, expand1), big_outs[2:]):
        target[...] = source[...].astype(f32)

    @pl.when(pl.program_id(0) == 0)
    def _():
        row, width = 0, small.shape[1]
        last = small_outs[-1]
        parts = last.shape[1] // width
        me = lax.axis_index("tensor")
        for target in small_outs[:-1]:
            for q in range(target.shape[1] // width):
                target[:, q * width : (q + 1) * width] = small[row : row + 1, :].astype(f32)
                row += 1
        for q in range(parts):
            value = None
            for owner in range(group):
                at = row + owner * parts + q
                mine = jnp.where(me == owner, small[at : at + 1, :].astype(f32), 0.0)
                value = mine if value is None else value + mine
            last[:, q * width : (q + 1) * width] = value


def unpack(plan, gout, gin, gx, flat):
    width, ch, hid, out, group = plan.width, plan.channels, plan.hidden, plan.out, plan.group
    shape = partial(jax.ShapeDtypeStruct, dtype=f32)
    taps, steps = 9 * width, UNPACK_STEPS
    quarters = ch // width
    each = steps // quarters

    def rows_spec(size, start, columns=width):
        assert start % size == 0
        return pl.BlockSpec((size, columns), lambda i: (start // size + i, 0))

    lane = width // each
    in_specs = [
        pl.BlockSpec((PIECES, hid // steps, plan.piece), lambda i: (0, i, 0)),
        rows_spec(ch // steps, 0, hid),
        rows_spec(plan.early.rows // steps, 0, ch),
        *[rows_spec(taps // steps, plan.kernel_at[n]) for n in range(2)],
        *[rows_spec(ch // steps, plan.reduce_at[n]) for n in range(2)],
        *[rows_spec(lane, plan.expand_at[n]) for n in range(2)],
        pl.BlockSpec((128, width), lambda i: (plan.small_at // 128, 0)),
    ]
    expand_out = pl.BlockSpec((lane, width), lambda i: (i % each, i // each))
    smalls = [width] * 4 + [ch] * 2
    smalls = smalls + smalls + [out, hid]
    out_specs = [
        rows_spec(hid // steps, 0, out),
        rows_spec(ch // steps, 0, hid),
        rows_spec(plan.early.rows // steps, 0, ch),
        *[rows_spec(taps // steps, 0)] * 2,
        *[rows_spec(ch // steps, 0)] * 2,
        *[expand_out] * 2,
        *[pl.BlockSpec((1, size), lambda i: (0, 0)) for size in smalls],
    ]
    out_shape = [shape((hid, out)), shape((ch, hid)), shape((plan.early.rows, ch))]
    out_shape += [shape((taps, width))] * 2 + [shape((ch, width))] * 2 + [shape((width, ch))] * 2
    out_shape += [shape((1, size)) for size in smalls]
    return pl.pallas_call(
        partial(unpack_body, group), grid=(steps,), in_specs=in_specs, out_specs=out_specs, out_shape=out_shape
    )(gout, gin.reshape(ch, hid), gx, *[flat] * 7)


def shards(*args):
    patches, early, late = args[0], args[1:10], args[10:19]
    readin_weight, readin_bias, readout_weight, readout_bias, cotangent, span_start = args[19:]
    images, side, _, channels = patches.shape
    width, hidden, out = early[0].shape[1], readin_weight.shape[1], readout_weight.shape[1]
    group, ring = lax.axis_size("tensor"), lax.axis_size("dp")
    plan = Plan(images, side, channels, width, group, ring, hidden, out)
    chips, block, rows = plan.chips, plan.block, plan.rows

    def matrices(params):
        kernel = params[3].reshape(3, 3 * width, width)
        return [params[0], params[1][None], params[2][None], kernel, params[4][None], params[5][None],
                params[6], params[7][None], params[8][None]]

    inputs = {"starts": span_start, "xs": patches.reshape(-1, channels)}
    inputs |= {f"early{k}": item for k, item in enumerate(matrices(early))}
    inputs |= {f"late{k}": item for k, item in enumerate(matrices(late))}
    inputs |= {"win": readin_weight, "bin": readin_bias.reshape(-1, 128), "wout": readout_weight,
               "bout": readout_bias.reshape(-1, 128), "cot": cotangent}
    streamed = {name: inputs[name].shape for name in STREAMED}
    inputs = {name + "_in" if name in streamed else name: item for name, item in inputs.items()}
    quarter = plan.flat // group
    gflat = (2, chips, PIECES, plan.flat_piece, width) if plan.ring else (plan.flat, width)
    outputs = {
        "projected": (block, out),
        "gx": (plan.early.rows, channels),
        "gout": (PIECES, hidden, plan.piece),
        "gin": (PIECES, plan.slab, hidden),
        "gflat": gflat,
        "gall": (group, PIECES, block, plan.piece),
        "rpair": (chips, block, out),
        "rfar": (max(chips - 1, 1), block, out),
        "tpair": (chips, block, channels),
        "tfar": (chips - 1, block, channels),
        "fpair": (plan.flat // 2, width),
        "ffar": (2, quarter // 2, width),
    }
    hops = RING - 1
    early_rows, late_rows = plan.early.rows, plan.late.rows
    low = {
        **streamed,
        "tok": (group, block, channels),
        "act": (rows, hidden),
        "slope": (rows, hidden),
        "turned": (max(hidden, 2 * block), rows),
        "gbuf": (2, 2, rows, plan.piece),
        "held": (2, hops, hidden, plan.piece),
        "first": (2, hidden, plan.piece),
        "wbuf": (4, hidden, plan.piece),
        "rbuf": (chips, block, out),
        "tsend": (chips, block, channels),
        "held2": (2, hops, plan.slab, hidden),
        "first2": (2, plan.slab, hidden),
        "held3": (2, hops, plan.flat_piece, width),
        "first3": (2, plan.flat_piece, width),
        "flat": (plan.flat, width),
    }
    wide = {
        "pool": (late_rows, channels),
        "gpool": (late_rows, channels),
        "ered": (early_rows, width),
        "econv": (early_rows, width),
        "lred": (late_rows, width),
        "lconv": (late_rows, width),
        "big": (max(plan.early.padded, rows), max(3 * width, hidden)),
        "small": (64, width),
        "outbias": (PIECES, plan.piece),
        "inbias": (1, hidden),
        "bin_wide": (1, hidden),
        "bout_wide": (1, out),
        "acc0": (channels, width),
        "acc1": (1, width),
        "acc2": (1, width),
        "acc3": (9 * width, width),
        "acc4": (1, width),
        "acc5": (1, width),
        "acc6": (width, channels),
        "acc7": (1, channels),
        "acc8": (1, channels),
    }
    remote = {
        "cx": (chips - 1, RING, 2),
        "cc": (chips, RING, 2),
        "tx": (chips - 1, images),
        "tc": (chips, images),
        "rp": (chips,),
        "rx": (chips - 1,),
        "gc": (chips,),
        "gx_": (chips - 1,),
        "fp": (1,),
        "fx": (chips - 1,),
        "ax": (chips - 1, 2, RING),
        "ac": (chips, 2, RING),
    }
    copies = {f"{name}_{end}": size for name, size in remote.items() for end in "sr"}
    copies |= {f"ring_{kind}": (SUBS + 2, 2, hops) for kind in ("rs", "rr", "gs", "gr")}
    copies |= {"ring_l": (SUBS + 2, 2), "load": (4,), "pload": (len(STREAMED),), "tload": (2, channels // 256), "gload": (2, 2, group), "wload": (4, 3), "aload": (2, 2, group + 1)}
    hbm, vmem = pl.BlockSpec(memory_space=pltpu.HBM), pl.BlockSpec(memory_space=pltpu.VMEM)
    kinds = {"starts": pl.BlockSpec(memory_space=pltpu.SMEM), "wout": hbm, "cot": hbm}
    kinds |= {name + "_in": hbm for name in STREAMED}
    scratch = [pltpu.VMEM(size, bf16) for size in low.values()]
    scratch += [pltpu.VMEM(size, f32) for size in wide.values()]
    scratch += [pltpu.SemaphoreType.DMA(size) for size in copies.values()]
    names = [*inputs, *outputs, *low, *wide, *copies]
    landed = pl.pallas_call(
        partial(mega, plan, names),
        out_shape=[jax.ShapeDtypeStruct(size, bf16) for size in outputs.values()],
        in_specs=[kinds.get(name, vmem) for name in inputs],
        out_specs=[hbm] * len(outputs),
        scratch_shapes=scratch,
        compiler_params=pltpu.CompilerParams(
            collective_id=0, has_side_effects=True, vmem_limit_bytes=67043328
        ),
    )(*inputs.values())
    projected, grad_x, gout, gin, flat = landed[:5]
    flat = flat.reshape(plan.flat, width)
    if not plan.ring:
        gout, gin = lax.psum(gout, "dp"), lax.psum(gin, "dp")
        flat = lax.psum(flat, ("dp", "tensor"))
    done = unpack(plan, gout, gin, grad_x, flat)
    grad_readout, grad_readin, grad_patches = done[:3]
    kernels, reduces, expands, smalls = done[3:5], done[5:7], done[7:9], done[9:]

    def grads(n):
        small = [item.reshape(-1) for item in smalls[6 * n : 6 * n + 6]]
        kernel = kernels[n].reshape(3, 3, width, width)
        return [reduces[n], small[0], small[1], kernel, small[2], small[3], expands[n], small[4], small[5]]

    return (
        projected,
        grad_patches.reshape(patches.shape),
        *grads(0),
        *grads(1),
        grad_readin,
        smalls[13].reshape(-1),
        grad_readout,
        smalls[12].reshape(-1),
    )


def solution(mesh):
    in_specs = (
        P(("dp", "tensor"), None, None, None),
        P(),
        P(),
        P(),
        P(),
        P(),
        P(),
        P(),
        P(),
        P(),
        P(),
        P(),
        P(),
        P(),
        P(),
        P(),
        P(),
        P(),
        P(),
        P(None, "tensor"),
        P("tensor"),
        P("tensor", None),
        P(),
        P(("dp", "tensor"), None),
        P(("dp", "tensor")),
    )
    out_specs = (
        P(("dp", "tensor"), None),
        P(("dp", "tensor"), None, None, None),
        P(),
        P(),
        P(),
        P(),
        P(),
        P(),
        P(),
        P(),
        P(),
        P(),
        P(),
        P(),
        P(),
        P(),
        P(),
        P(),
        P(),
        P(),
        P(None, "tensor"),
        P("tensor"),
        P("tensor", None),
        P(),
    )
    return jax.shard_map(shards, mesh=mesh, in_specs=in_specs, out_specs=out_specs, check_vma=False)
```
